32 devices in a mesh: pipe: 2 (over x), expert: 16 (over z, y, core).
Axes of the slice: x: 2, y: 2, z: 4, core: 2. Of those that a mesh axis runs over, the one named last changes fastest.
Arguments:
- tokens: bfloat16 [2, 2048, 7168], P('pipe', 'expert'), may hold values from -24 to 24
- grad_out: bfloat16 [2, 2048, 7168], P('pipe', 'expert'), may hold values from -6 to 6
- norm_gain: float32 [2, 7168], P('pipe'), may hold values from 0.25 to 1.75
- expert_ids: int32 [2, 2048, 2], P('pipe', 'expert'), may hold values from 0 to 3, all different within a row; in each aligned block of 128 rows (0 to 127, 128 to 255, ..., all dimensions but the last counted through in order) at most 80 rows name the same one
- gate_weights: float32 [2, 2048, 2], P('pipe', 'expert'), may hold values from 0.2 to 1
- w_gate: bfloat16 [2, 7168, 4096], P('pipe', None, 'expert'), may hold values from -0.0625 to 0.0625
- w_up: bfloat16 [2, 7168, 4096], P('pipe', None, 'expert'), may hold values from -0.0625 to 0.0625
- w_down: bfloat16 [2, 4096, 7168], P('pipe', 'expert'), may hold values from -0.1875 to 0.1875
Outputs:
- next_in: bfloat16 [2, 2048, 7168], P('pipe', 'expert')
- prev_grad: bfloat16 [2, 2048, 7168], P('pipe', 'expert')
The draws below stay inside these ranges and needn't reach their ends.
Inputs may be any that keep to these rules, and one draw needn't show every extreme that they name: `expert_ids`: each token's 2 ids differ. In the rows of one device (aligned blocks of 128 rows of each section) no expert is named by more than 80 rows.
All inputs are finite; a program needn't handle non-finite values.
Results may differ from the reference program's by a relative error of at most 0.0048.
Values may be sent and summed in bfloat16 or wider, within the bound.
A program may use at most 192 MiB of HBM per device.

```python
import math
import jax
import jax.numpy as jnp
import numpy as np
from jax import lax

D = 7168
EH = 1024
SLICES = 4
TOP = 2
TOK_DEV = 128
FFD = 256
EXPERTS = 4
TOKENS = 2048
CAP = 80
N_PIPE = 2
N_EXPERT = 16


def draw_tokens(key, part):
    base_key = jax.random.fold_in(key, 11)
    keys = jax.random.split(base_key, 3)
    column_scale = jnp.exp(jax.random.uniform(keys[1], (1, 1, D), jnp.float32, math.log(0.3), math.log(3.0)))
    row_scale = jnp.exp(jax.random.uniform(keys[2], (N_PIPE, TOKENS, 1), jnp.float32, math.log(0.5), math.log(2.0)))
    base = jnp.clip(jax.random.normal(keys[0], (N_PIPE, TOKENS, D), jnp.float32), -4.0, 4.0)
    return (base * column_scale * row_scale).astype(jnp.bfloat16)


def shard_levels(stream_key, extent, cuts, low, top_value):
    def one(position, shards_of):
        heights = jax.random.uniform(jax.random.fold_in(jax.random.fold_in(stream_key, 6), position), (shards_of,), jnp.float32, low / len(cuts), top_value / len(cuts))
        return jnp.repeat(jnp.exp(heights), extent[position] // shards_of).reshape((-1,) + (1,) * (len(extent) - position - 1))

    factor_of = one(*cuts[0])
    for cut in cuts[1:]:
        factor_of = factor_of * one(*cut)
    return factor_of


def shared_out(key, own, number, rows, number_of, top, most, lean):
    sequence = jax.random.permutation(key, number_of)
    packed, ordinary = load_shares(number_of, rows * top, most, lean, True), load_shares(number_of, rows * top, most, lean, False)
    places = jnp.arange(number_of)

    def named(tallies, rotation):
        used = int((tallies > 0).sum())
        fixed = max(1, used // 4)
        moved = fixed + (places - fixed + rotation * (used - fixed)) % max(1, number_of - fixed)
        return jnp.zeros((number_of,), jnp.int32).at[sequence[jnp.where(places < fixed, places, moved)]].set(jnp.asarray(tallies, jnp.int32))

    tallies = jnp.where(number % 4 == 0, named(packed, number // 4), named(ordinary, number - number // 4 - 1))
    mixed = jax.random.permutation(jax.random.fold_in(own, 3), number_of)
    donor, sink = mixed[0:number_of // 2 * 2:2], mixed[1:number_of // 2 * 2:2]
    slack = jnp.minimum(tallies[donor] - 1, most - tallies[sink]) // 2
    slack = jnp.where((donor == sequence[0]) | (sink == sequence[0]) | (tallies[sink] == 0), 0, jnp.maximum(slack, 0))
    moved = jax.random.randint(jax.random.fold_in(own, 4), (number_of // 2,), 0, 1 << 20) % (slack + 1)
    tallies = tallies.at[donor].add(-moved).at[sink].add(moved)
    labels = jnp.searchsorted(jnp.cumsum(tallies), jnp.arange(rows * top), side="right").astype(jnp.int32)
    table = labels.reshape(top, rows).T
    table = table[jax.random.permutation(jax.random.fold_in(own, 1), rows)]
    rotation = jax.random.randint(jax.random.fold_in(own, 2), (rows, 1), 0, top)
    return jnp.take_along_axis(table, (jnp.arange(top)[None, :] + rotation) % top, axis=1)


def load_shares(count, total, reach, skew, full):
    weights = [(1 << 20) // math.isqrt(grade ** skew) + 1 for grade in range(1, count + 1)]
    largest = reach if full else min(reach, max(-(-total // count), total * weights[0] // sum(weights)))
    least = 1 if total - largest >= count - 1 else 0
    holding, surplus = [largest] + [least] * (count - 1), total - largest - least * (count - 1)
    while surplus > 0:
        candidates = [i for i in range(1, count) if holding[i] < largest] or [i for i in range(1, count) if holding[i] < reach]
        pool, left = sum([weights[i] for i in candidates]), surplus
        for i in candidates:
            extra = min(reach - holding[i], max(1, left * weights[i] // pool), surplus)
            holding[i] = holding[i] + extra
            surplus = surplus - extra
    return np.array(holding)


def noise(rng, extent, deviation, limit, pieces=(), kind=jnp.bfloat16):
    entries = jax.random.normal(rng, extent, jnp.float32) * deviation
    if len(pieces) > 0:
        entries = shard_levels(rng, extent, pieces, -0.22, 0.18) * entries
    return jnp.clip(entries, min=-limit, max=limit).astype(kind)


def setup_inputs(seed: int = 0) -> dict:
    key_list = jax.random.split(jax.random.key(seed), 9)
    tokens = draw_tokens(jax.random.fold_in(key_list[8], 71), 0)
    grad_out = noise(key_list[1], (N_PIPE, TOKENS, D), 1.0, 6.0, ((0, 2), (1, 16)))
    norm_gain = jnp.clip(1.0 + 0.15 * jax.random.normal(key_list[2], (N_PIPE, D), jnp.float32), 0.25, 1.75)
    expert_ids_keys = jax.random.split(jax.random.fold_in(key_list[3], 1), N_PIPE * TOKENS // TOK_DEV)
    expert_ids_turns = jax.random.permutation(jax.random.fold_in(key_list[3], 3), N_PIPE * TOKENS // TOK_DEV)
    expert_ids = jax.vmap(lambda own, number: shared_out(jax.random.fold_in(key_list[3], 2), own, number, TOK_DEV, EXPERTS, TOP, CAP, 2))(expert_ids_keys, expert_ids_turns).reshape((N_PIPE, TOKENS, TOP))
    gate_weights = jnp.clip(jnp.exp(math.log(1.0) - 1.609438 * jax.random.uniform(key_list[4], (N_PIPE, TOKENS, TOP), jnp.float32) ** shard_levels(key_list[4], (N_PIPE, TOKENS, TOP), ((0, 2), (1, 16)), -0.2, 0.2)), 0.2, 1.0)
    w_gate = noise(key_list[5], (N_PIPE, D, EXPERTS * EH), D ** -0.5, 0.0625, ((0, 2), (2, 16)))
    w_up = noise(key_list[6], (N_PIPE, D, EXPERTS * EH), D ** -0.5, 0.0625, ((0, 2), (2, 16)))
    w_down = noise(key_list[7], (N_PIPE, EXPERTS * EH, D), EH ** -0.5, 0.1875, ((0, 2), (1, 16)))
    return {"tokens": tokens, "grad_out": grad_out, "norm_gain": norm_gain, "expert_ids": expert_ids, "gate_weights": gate_weights, "w_gate": w_gate, "w_up": w_up, "w_down": w_down}


EPSILON = 1e-06

def transpose_dot(left_arr, right_arr):
    return lax.dot_general(left_arr, right_arr, (((1,), (1,)), ((), ())), preferred_element_type=jnp.float32)

def expert_apply(rows_in, rows_grad, gate_cols, up_cols, down_rows):
    gate_pre = jnp.dot(rows_in, gate_cols, preferred_element_type=jnp.float32)
    up_pre = jnp.dot(rows_in, up_cols, preferred_element_type=jnp.float32)
    sigmoid_gate = jax.nn.sigmoid(gate_pre)
    swish_gate = gate_pre * sigmoid_gate
    hidden = (swish_gate * up_pre).astype(jnp.bfloat16)
    part_out = jnp.dot(hidden, down_rows, preferred_element_type=jnp.float32).astype(jnp.bfloat16)
    grad_hidden = transpose_dot(rows_grad, down_rows)
    grad_gate = (grad_hidden * up_pre * sigmoid_gate * (1.0 + gate_pre * (1.0 - sigmoid_gate))).astype(jnp.bfloat16)
    grad_up = (grad_hidden * swish_gate).astype(jnp.bfloat16)
    part_grad = (transpose_dot(grad_gate, gate_cols) + transpose_dot(grad_up, up_cols)).astype(jnp.bfloat16)
    return (part_out, part_grad)

def section_layer(tokens, grad_out, gain_row, route_ids, route_weights, gate_all, up_all, down_all):
    token_count = tokens.shape[0]
    values = tokens.astype(jnp.float32)
    inverse = lax.rsqrt(lax.optimization_barrier(jnp.mean(values * values, axis=-1, keepdims=True)) + EPSILON)
    gain_wide = gain_row.astype(jnp.float32)[None, :]
    normed = (values * inverse * gain_wide).astype(jnp.bfloat16)
    flat_ids = route_ids.reshape(-1).astype(jnp.int32)
    pair_count = flat_ids.shape[0]
    sorted_pairs = jnp.argsort(flat_ids, stable=True).astype(jnp.int32)
    counts = lax.optimization_barrier(jnp.sum((flat_ids[:, None] == jnp.arange(EXPERTS, dtype=jnp.int32)[None, :]).astype(jnp.int32), axis=0))
    starts = (jnp.cumsum(counts) - counts).astype(jnp.int32)
    most_rows = N_EXPERT * CAP
    padded_pairs = jnp.concatenate([sorted_pairs, jnp.full((most_rows,), pair_count, jnp.int32)])
    normed_pad = jnp.concatenate([normed, jnp.zeros((1, D), jnp.bfloat16)])
    grad_pad = jnp.concatenate([grad_out, jnp.zeros((1, D), jnp.bfloat16)])

    def one_expert(expert_index):
        picked = lax.dynamic_slice_in_dim(padded_pairs, starts[expert_index], most_rows)
        live_rows = jnp.arange(most_rows, dtype=jnp.int32) < counts[expert_index]
        picked = jnp.where(live_rows, picked, pair_count).astype(jnp.int32)
        row_token = (picked // TOP).astype(jnp.int32)
        rows_in = normed_pad[row_token]
        rows_grad = grad_pad[row_token]
        sum_out = jnp.zeros((most_rows, D), jnp.float32)
        sum_grad = jnp.zeros((most_rows, D), jnp.float32)
        for slice_index in range(SLICES):
            column = (expert_index * EH + slice_index * FFD).astype(jnp.int32)
            gate_cols = lax.dynamic_slice_in_dim(gate_all, column, FFD, 1)
            up_cols = lax.dynamic_slice_in_dim(up_all, column, FFD, 1)
            down_rows = lax.dynamic_slice_in_dim(down_all, column, FFD, 0)
            part_out, part_grad = expert_apply(rows_in, rows_grad, gate_cols, up_cols, down_rows)
            sum_out = sum_out + part_out.astype(jnp.float32)
            sum_grad = sum_grad + part_grad.astype(jnp.float32)
        return (picked, sum_out, sum_grad)
    picked, outs, grads = lax.map(one_expert, jnp.arange(EXPERTS, dtype=jnp.int32))
    flat_pick = picked.reshape(-1)
    pair_out = jnp.zeros((pair_count + 1, D), jnp.float32).at[flat_pick].add(outs.reshape(-1, D))
    pair_grad = jnp.zeros((pair_count + 1, D), jnp.float32).at[flat_pick].add(grads.reshape(-1, D))
    weights = route_weights.astype(jnp.float32)[:, :, None]
    mixed_rows = lax.optimization_barrier(jnp.sum(pair_out[:pair_count].reshape(token_count, TOP, D) * weights, axis=1))
    grad_normed = lax.optimization_barrier(jnp.sum(pair_grad[:pair_count].reshape(token_count, TOP, D) * weights, axis=1))
    layer_out = (values + mixed_rows).astype(jnp.bfloat16)
    scaled = grad_normed * gain_wide
    cubed = inverse * inverse * inverse
    grad_in = (grad_out.astype(jnp.float32) + inverse * scaled - values * cubed * lax.optimization_barrier(jnp.mean(scaled * values, axis=-1, keepdims=True))).astype(jnp.bfloat16)
    return (layer_out, grad_in)

def reference(tokens, grad_out, norm_gain, expert_ids, gate_weights, w_gate, w_up, w_down):
    outputs = []
    gradients = []
    for section in range(N_PIPE):
        layer_out, grad_in = section_layer(tokens[section], grad_out[section], norm_gain[section], expert_ids[section], gate_weights[section], w_gate[section], w_up[section], w_down[section])
        outputs.append(layer_out)
        gradients.append(grad_in)
    stacked_out = jnp.stack(outputs)
    stacked_grad = jnp.stack(gradients)
    return (jnp.roll(stacked_out, 1, axis=0), jnp.roll(stacked_grad, -1, axis=0))
```

```python
import jax
import jax.numpy as jnp
from jax import lax
from jax.experimental import pallas as pl
from jax.experimental.pallas import tpu as pltpu
from jax.sharding import PartitionSpec as P

SLICES = 4
EPSILON = 1e-06
BF16 = jnp.bfloat16
F32 = jnp.float32


def move(value, pipe_steps, expert_map):
    pipes, devices = lax.axis_size("pipe"), lax.axis_size("expert")
    pairs = [
        (p * devices + d, ((p + pipe_steps) % pipes) * devices + expert_map(d))
        for p in range(pipes)
        for d in range(devices)
    ]
    return lax.ppermute(value, ("pipe", "expert"), pairs)


def dot_nt(left_arr, right_arr):
    return lax.dot_general(
        left_arr, right_arr, (((1,), (1,)), ((), ())), preferred_element_type=F32
    )


def dot_nn(left_arr, right_arr):
    return jnp.dot(left_arr, right_arr, preferred_element_type=F32)


def tile_of(width):
    for tile in (1024, 512, 256, 128):
        if width % tile == 0:
            return tile
    return width


MESH = pl.DeviceIdType.MESH
ANY = pl.BlockSpec(memory_space=pl.ANY)


def sections():
    pipe, pipes = lax.axis_index("pipe"), lax.axis_size("pipe")
    return pipe, lax.rem(pipe + 1, pipes), lax.rem(pipe + pipes - 1, pipes)


def greet(partners):
    barrier = pltpu.get_barrier_semaphore()
    for partner in partners:
        pl.semaphore_signal(barrier, inc=1, device_id=partner, device_id_type=MESH)
    pl.semaphore_wait(barrier, len(partners))


VMEM = 62 * 1024 * 1024


def layer(picker, inverse, gain, gate, up, down, tokens, grad_rows,
          gain_prev, inverse_prev, pick_next, wt_next, pick_prev, wt_prev):
    rows = picker.shape[0]
    experts, _, capacity = pick_next.shape
    width = tokens.shape[1]
    ffd = down.shape[0]
    token_count, top = wt_next.shape
    devices, pipes = lax.axis_size("expert"), lax.axis_size("pipe")
    tile = tile_of(width)
    tiles = width // tile

    def kernel(pick, inv_own, gain_own, wg, wu, wd, tok, grd, gain, inv, pn, wn, pp, wp,
               next_ref, prev_ref, ag, au, ad,
               ri, rg, si, sg, tn, tp, gp, recv_o, recv_g, scaled, acc_g, acc_u, acc_h, hid, gg, ug,
               buf_g, buf_u, buf_d,
               far_s, far_r, cross_s, cross_r, near_s, near_r, rows_s, rows_r, tok_s, tok_r,
               load_sem, send, recv):
        pipe, after, ahead = sections()
        me = lax.axis_index("expert")
        place = lax.rem(me, SLICES)
        far = me - place + lax.rem(place + 2, SLICES)
        near = me + 1 - 2 * lax.rem(me, 2)
        others = [lax.rem(me + SLICES * s, devices) for s in range(1, experts)]
        homes = [lax.rem(me + devices - SLICES * s, devices) for s in range(experts)]
        greet(
            [(pipe, d) for d in others]
            + [(pipe, far), (pipe, near)]
            + [(p, d) for p in (after, ahead) for d in homes]
        )
        weights = ((wg, ag, buf_g), (wu, au, buf_u), (wd, ad, buf_d))
        stages = (ri, rg)

        def remote(source, target, send_sem, recv_sem, device):
            return pltpu.make_async_remote_copy(
                src_ref=source, dst_ref=target, send_sem=send_sem, recv_sem=recv_sem,
                device_id=device, device_id_type=MESH,
            )

        def cols_of(i):
            return pl.ds(pl.multiple_of(i * tile, tile), tile)

        def part(ref, which, i):
            return ref.at[cols_of(i), :] if which < 2 else ref.at[:, cols_of(i)]

        def far_copy(which, i):
            own, full, _ = weights[which]
            return remote(
                part(own, which, i), part(full.at[1], which, i),
                far_s.at[which, i], far_r.at[which, i], (pipe, far),
            )

        def cross_copy(which, i):
            full = weights[which][1]
            return remote(
                part(full.at[1], which, i), part(full.at[2], which, i),
                cross_s.at[which, i], cross_r.at[which, i], (pipe, near),
            )

        def near_copy(which):
            own, full, _ = weights[which]
            return remote(own, full.at[0], near_s.at[which], near_r.at[which], (pipe, near))

        def row_copy(which, i, s):
            return remote(
                (si, sg)[which].at[s - 1, :, cols_of(i)], stages[which].at[s, :, cols_of(i)],
                rows_s.at[which, i, s - 1], rows_r.at[which, i, s - 1], (pipe, others[s - 1]),
            )

        def token_copies():
            moves = [(tok, tn, after), (grd, gp, ahead), (tok, tp, ahead)]
            return [
                remote(source, target, tok_s.at[n], tok_r.at[n], (device, me))
                for n, (source, target, device) in enumerate(moves)
            ]

        def loads(which, i):
            own, full, buf = weights[which]
            slot = lax.rem(i, 2)
            return [
                pltpu.make_async_copy(
                    part(own if j == 0 else full.at[j - 1], which, i),
                    buf.at[slot, j],
                    load_sem.at[which, slot, j],
                )
                for j in range(SLICES)
            ]

        def load(kinds, i):
            for which in kinds:
                for copy in loads(which, i):
                    copy.start()

        def loaded(kinds, i):
            for which in kinds:
                for copy in loads(which, i):
                    copy.wait()

        def result_copy(which, i, s):
            return remote(
                stages[which].at[s, :, cols_of(i)], (recv_o, recv_g)[which].at[s, :, cols_of(i)],
                send.at[which, i, s], recv.at[which, i, s], ((after, ahead)[which], homes[s]),
            )

        def ship(which, i, total):
            for s in range(experts):
                stages[which][s, :, cols_of(i)] = total[s * capacity : (s + 1) * capacity].astype(BF16)
            for s in range(experts):
                result_copy(which, i, s).start()

        def send_rows(which, i):
            cols = cols_of(i)
            value = tok[:, cols].astype(F32) * inv_own[...] * gain_own[:, cols] if which == 0 else grd[:, cols]
            slots = dot_nn(pick[...], value.astype(BF16))
            stages[which][0, :, cols] = slots[:capacity].astype(BF16)
            for s in range(1, experts):
                (si, sg)[which][s - 1, :, cols] = slots[s * capacity : (s + 1) * capacity].astype(BF16)
            for s in range(experts - 1, 0, -1):
                row_copy(which, i, s).start()

        def send_far(kinds, i):
            for which in kinds:
                far_copy(which, i).start()

        def tile_rows(which, i):
            return stages[which][:, :, cols_of(i)].reshape(rows, tile)

        def piece(j):
            return slice(j * ffd, (j + 1) * ffd)

        first_far, first_down = min(2, tiles), min(4, tiles)
        for i in range(first_far):
            send_far((0, 1), i)

        @pl.loop(0, tiles)
        def _(i):
            send_rows(0, i)

        for which in range(3):
            near_copy(which).start()
        for copy in token_copies():
            copy.start()
        acc_g[...] = jnp.zeros_like(acc_g)
        acc_u[...] = jnp.zeros_like(acc_u)
        acc_h[...] = jnp.zeros_like(acc_h)
        near_copy(0).wait()
        near_copy(1).wait()

        def pipeline(kinds, arrive, compute):
            @pl.loop(0, tiles + 2)
            def _(i):
                @pl.when(i < tiles)
                def _():
                    arrive(i)
                    for which in kinds:
                        far_copy(which, i).wait()
                        cross_copy(which, i).start()

                @pl.when((i >= 1) & (i <= tiles))
                def _():
                    for which in kinds:
                        cross_copy(which, i - 1).wait()
                    load(kinds, i - 1)

                @pl.when(i >= 2)
                def _():
                    loaded(kinds, i - 2)
                    compute(i - 2)

        def arrive_first(i):
            send_rows(1, i)

            @pl.when(i + first_far < tiles)
            def _():
                send_far((0, 1), i + first_far)

            @pl.when(i == tiles - 1)
            def _():
                for n in range(first_down):
                    send_far((2,), n)

        def compute_first(i):
            for s in range(1, experts):
                row_copy(0, i, s).wait()
            slot = lax.rem(i, 2)
            block = tile_rows(0, i)
            for j in range(SLICES):
                acc_g[:, piece(j)] += dot_nn(block, buf_g[slot, j])
                acc_u[:, piece(j)] += dot_nn(block, buf_u[slot, j])

        pipeline((0, 1), arrive_first, compute_first)

        for j in range(SLICES):
            gate_pre = acc_g[:, piece(j)]
            hid[:, piece(j)] = (gate_pre * jax.nn.sigmoid(gate_pre) * acc_u[:, piece(j)]).astype(BF16)
        near_copy(2).wait()

        def arrive_down(i):
            @pl.when(i + first_down < tiles)
            def _():
                send_far((2,), i + first_down)

        def compute_down(i):
            slot = lax.rem(i, 2)
            total = dot_nn(hid[:, piece(0)], buf_d[slot, 0])
            for j in range(1, SLICES):
                total += dot_nn(hid[:, piece(j)], buf_d[slot, j])
            ship(0, i, total)
            for s in range(1, experts):
                row_copy(1, i, s).wait()
            block = tile_rows(1, i)
            for j in range(SLICES):
                acc_h[:, piece(j)] += dot_nt(block, buf_d[slot, j])

        pipeline((2,), arrive_down, compute_down)

        load((0, 1), 0)
        for j in range(SLICES):
            gate_pre, up_pre, grad_hidden = acc_g[:, piece(j)], acc_u[:, piece(j)], acc_h[:, piece(j)]
            sig = jax.nn.sigmoid(gate_pre)
            gg[:, piece(j)] = (grad_hidden * up_pre * sig * (1.0 + gate_pre * (1.0 - sig))).astype(BF16)
            ug[:, piece(j)] = (grad_hidden * (gate_pre * sig)).astype(BF16)

        @pl.loop(0, tiles)
        def _(i):
            @pl.when(i + 1 < tiles)
            def _():
                load((0, 1), i + 1)

            loaded((0, 1), i)
            slot = lax.rem(i, 2)
            total = dot_nt(gg[:, piece(0)], buf_g[slot, 0]) + dot_nt(ug[:, piece(0)], buf_u[slot, 0])
            for j in range(1, SLICES):
                total += dot_nt(gg[:, piece(j)], buf_g[slot, j]) + dot_nt(ug[:, piece(j)], buf_u[slot, j])
            ship(1, i, total)

        def picked(target, pick, scale, cols):
            total = dot_nn(pick[0], target[0, :, cols])
            for s in range(1, experts):
                total += dot_nn(pick[s], target[s, :, cols])
            value = total[:token_count] * scale[:, 0:1]
            for n in range(1, top):
                value += total[n * token_count : (n + 1) * token_count] * scale[:, n : n + 1]
            return value

        for copy in token_copies():
            copy.wait()

        @pl.loop(0, tiles)
        def _(i):
            cols = cols_of(i)
            for s in range(experts):
                result_copy(0, i, s).wait()
            next_ref[:, cols] = (tn[:, cols].astype(F32) + picked(recv_o, pn, wn, cols)).astype(BF16)

        def finish(i, mean):
            cols = cols_of(i)
            for s in range(experts):
                result_copy(1, i, s).wait()
            value = picked(recv_g, pp, wp, cols) * gain[:, cols]
            scaled[:, cols] = value
            return mean + jnp.sum(value * tp[:, cols].astype(F32), axis=1, keepdims=True)

        mean = lax.fori_loop(0, tiles, finish, jnp.zeros((token_count, 1), F32)) / width
        inverse = inv[...]
        factor = inverse * inverse * inverse * mean

        @pl.loop(0, tiles)
        def _(i):
            cols = cols_of(i)
            prev_ref[:, cols] = (
                gp[:, cols].astype(F32) + inverse * scaled[:, cols] - tp[:, cols].astype(F32) * factor
            ).astype(BF16)

    three = lambda value: jax.ShapeDtypeStruct((3,) + value.shape, value.dtype)
    in_vmem = pl.BlockSpec(memory_space=pltpu.VMEM)
    result = jax.ShapeDtypeStruct((token_count, width), BF16)
    row_block = pltpu.VMEM((experts, capacity, width), BF16)
    token_block = pltpu.VMEM((token_count, width), BF16)
    wide = (rows, SLICES * ffd)
    dma = pltpu.SemaphoreType.DMA
    return pl.pallas_call(
        kernel,
        in_specs=[in_vmem] * 3 + [ANY] * 3 + [in_vmem] * 8,
        out_specs=[in_vmem] * 2 + [ANY] * 3,
        out_shape=[result] * 2 + [three(gate), three(up), three(down)],
        scratch_shapes=[row_block] * 2
        + [pltpu.VMEM((experts - 1, capacity, width), BF16)] * 2
        + [token_block] * 3
        + [row_block] * 2
        + [pltpu.VMEM((token_count, width), F32)]
        + [pltpu.VMEM(wide, F32)] * 3
        + [pltpu.VMEM(wide, BF16)] * 3
        + [pltpu.VMEM((2, SLICES, tile, ffd), BF16)] * 2
        + [pltpu.VMEM((2, SLICES, ffd, tile), BF16)]
        + [dma((3, tiles))] * 4
        + [dma((3,))] * 2
        + [dma((2, tiles, experts - 1))] * 2
        + [dma((3,))] * 2
        + [dma((3, 2, SLICES))]
        + [dma((2, tiles, experts))] * 2,
        compiler_params=pltpu.CompilerParams(
            collective_id=0, has_side_effects=True, vmem_limit_bytes=VMEM
        ),
        name="layer",
    )(picker, inverse, gain, gate, up, down, tokens, grad_rows,
      gain_prev, inverse_prev, pick_next, wt_next, pick_prev, wt_prev)[:2]


LANES = 128
AHEAD = 8
FAR_AHEAD = 4
DOWN_AHEAD = 8
RELAY_LAG = 1
FINISH_LAG = 2


def relay_layer(table, gain, gate, up, down, tokens, grad_rows, capacity, top):
    experts = 4
    token_count, width = tokens.shape
    ffd = down.shape[0]
    hidden = SLICES * ffd
    rows = experts * capacity
    devices = lax.axis_size("expert")
    tile = min(512, tile_of(width))
    tiles = width // tile
    units = 2 * tiles

    def kernel(tab, gain_ref, wg, wu, wd, tok, grd,
               next_ref, prev_ref, ag, au, ad,
               own, stage, nbuf, rbuf, raw, cbuf, obuf, info, square, pick, back, scale, coef,
               rho_out, rho_in, acc_g, acc_u, acc_h, hid, gg, ug, buf_g, buf_u, buf_d,
               own_l, raw_s, raw_r, info_s, info_r, nb_s, nb_r, ret_s, ret_r, cmb_s, cmb_r,
               rho_s, rho_r, out_s, out_r, far_s, far_r, cross_s, cross_r, near_s, near_r, load_sem):
        pipe, after, ahead = sections()
        me = lax.axis_index("expert")
        place = lax.rem(me, SLICES)
        mine = lax.div(me, SLICES)
        half = lax.div(mine, 2)
        outer_index = 1 - lax.rem(lax.div(mine + 1, 2), 2)
        inner = outer_index == 0
        outer = outer_index == 1
        far = me - place + lax.rem(place + 2, SLICES)
        near = me + 1 - 2 * lax.rem(me, 2)

        def device_of(expert):
            return (pipe, expert * SLICES + place)

        pair = mine + 1 - 2 * lax.rem(mine, 2)
        opposite = [2 - half, 3 - 3 * half]
        greet(
            [(pipe, lax.rem(me + SLICES * s, devices)) for s in range(1, experts)]
            + [(pipe, far), (pipe, near), (after, me), (ahead, me)]
        )
        weights = ((wg, ag, buf_g), (wu, au, buf_u), (wd, ad, buf_d))

        def remote(source, target, send_sem, recv_sem, device):
            return pltpu.make_async_remote_copy(
                src_ref=source, dst_ref=target, send_sem=send_sem, recv_sem=recv_sem,
                device_id=device, device_id_type=MESH,
            )

        def cols_of(i):
            return pl.ds(pl.multiple_of(i * tile, tile), tile)

        def part(ref, which, i):
            return ref.at[cols_of(i), :] if which < 2 else ref.at[:, cols_of(i)]

        def far_copy(which, i):
            weight, full, _ = weights[which]
            return remote(
                part(weight, which, i), part(full.at[1], which, i),
                far_s.at[which], far_r.at[which, i], (pipe, far),
            )

        def cross_copy(which, i):
            full = weights[which][1]
            return remote(
                part(full.at[1], which, i), part(full.at[2], which, i),
                cross_s.at[which], cross_r.at[which, i], (pipe, near),
            )

        def near_copy(which):
            weight, full, _ = weights[which]
            return remote(weight, full.at[0], near_s.at[which], near_r.at[which], (pipe, near))

        def loads(which, i):
            weight, full, buf = weights[which]
            slot = lax.rem(i, 2)
            return [
                pltpu.make_async_copy(
                    part(weight if j == 0 else full.at[j - 1], which, i),
                    buf.at[slot, j],
                    load_sem.at[which, slot, j],
                )
                for j in range(SLICES)
            ]

        def load(kinds, i):
            for which in kinds:
                for copy in loads(which, i):
                    copy.start()

        def loaded(kinds, i):
            for which in kinds:
                for copy in loads(which, i):
                    copy.wait()

        def split(u):
            return lax.div(u, tiles), lax.rem(u, tiles)

        def raw_copy(source, which, i):
            return remote(
                source, raw.at[which, i, outer_index], raw_s, raw_r.at[which, i, outer_index],
                device_of(opposite[0]),
            )

        def raw_start(u):
            which, i = split(u)
            raw_copy(own.at[which, :, cols_of(i)], which, i).start()

        def raw_wait(which, i, n):
            block = raw.at[which, i, n]
            remote(block, block, raw_s, raw_r.at[which, i, n], device_of(opposite[0])).wait_recv()

        def info_copy():
            return remote(
                info.at[0], info.at[1 + outer_index], info_s, info_r.at[outer_index], device_of(opposite[0])
            )

        def info_wait(n):
            block = info.at[1 + n]
            remote(block, block, info_s, info_r.at[n], device_of(opposite[0])).wait_recv()

        def nb_copy(which, i, blocks):
            return remote(
                nbuf.at[which, i, pl.ds(0, blocks)], stage.at[which, i, pl.ds(1, blocks)],
                nb_s, nb_r.at[which, i], device_of(pair),
            )

        def ret_copy(which, i, blocks):
            return remote(
                stage.at[which, i, pl.ds(1, blocks)], rbuf.at[which, i, pl.ds(0, blocks)],
                ret_s, ret_r.at[which, i], device_of(pair),
            )

        def cmb_copy(which, i, n):
            return remote(
                raw.at[which, i, n], cbuf.at[which, i], cmb_s, cmb_r.at[which, i], device_of(opposite[n])
            )

        def out_copy(which, i):
            return remote(
                obuf.at[which, i], (next_ref, prev_ref)[which].at[:, cols_of(i)],
                out_s.at[which], out_r.at[which], ((after, ahead)[which], me),
            )

        def rho_copies():
            places = (1, 2 + outer_index, 2 + outer_index)
            targets = (pair, opposite[0], opposite[1])
            return [
                remote(rho_out.at[n + 1], rho_in.at[places[n]], rho_s.at[n], rho_r.at[places[n]], device_of(targets[n]))
                for n in range(3)
            ]

        def rho_wait(n):
            block = rho_in.at[n]
            remote(block, block, rho_s.at[0], rho_r.at[n], device_of(pair)).wait_recv()

        own_loads = [
            pltpu.make_async_copy(source, own.at[n], own_l.at[n]) for n, source in enumerate((tok, grd))
        ]

        def piece(j):
            return slice(j * ffd, (j + 1) * ffd)

        for copy in own_loads:
            copy.start()
        first_raw = min(2, tiles)
        for i in range(min(FAR_AHEAD, tiles)):
            for which in (0, 1):
                far_copy(which, i).start()
            if i < first_raw:
                raw_copy(tok.at[:, cols_of(i)], 0, i).start()
        near_copy(0).start()
        near_copy(1).start()

        lane = lax.broadcasted_iota(jnp.int32, (token_count, LANES), 1)
        lane_value = lane.astype(F32)

        def full_of(n):
            square[...] = jnp.zeros_like(square)
            square[: info.shape[1]] = info[n]
            return square[...].T

        def column(full, index):
            return jnp.sum(jnp.where(lane == index, full, 0.0), axis=1, keepdims=True)

        def set_tables(n):
            full = full_of(n)
            slot = lax.broadcasted_iota(jnp.int32, (capacity, token_count), 0).astype(F32)
            slot_lane = lax.broadcasted_iota(jnp.int32, (token_count, capacity), 1).astype(F32)
            for k, expert in enumerate((mine, pair)):
                pick[n, k * capacity : (k + 1) * capacity] = (slot == info[n, pl.ds(expert, 1), :]).astype(BF16)
                back[n, k] = (slot_lane == column(full, expert)).astype(BF16)
                scale[n, k] = column(full, experts + expert)
            scale[n, 2] = column(full, 2 * experts)

        own_loads[0].wait()

        def add_squares(i, total):
            value = own[0, :, cols_of(i)].astype(F32)
            return total + jnp.sum(value * value, axis=1, keepdims=True)

        squares = lax.fori_loop(0, tiles, add_squares, jnp.zeros((token_count, 1), F32))
        inverse_own = lax.rsqrt(squares / width + EPSILON)
        hit = jnp.zeros((token_count, LANES), F32)
        weight_of = jnp.zeros((token_count, LANES), F32)
        for k in range(top):
            ids = tab[:, k : k + 1]
            hit += jnp.where(lane_value == ids, 1.0, 0.0)
            weight_of += jnp.where(lane_value == ids + experts, tab[:, top + k : top + k + 1], 0.0)
        earlier = (lane < lax.broadcasted_iota(jnp.int32, (token_count, LANES), 0)).astype(BF16)
        before = dot_nn(earlier, hit.astype(BF16))
        spot = jnp.where(hit > 0.5, before, -1.0)
        full_own = jnp.where(
            lane < experts, spot, jnp.where(lane < 2 * experts, weight_of, jnp.where(lane == 2 * experts, inverse_own, 0.0))
        )
        info[0] = full_own.T[: info.shape[1]]
        info_copy().start()
        own_loads[1].wait()
        for u in range(first_raw, min(AHEAD, units)):
            raw_start(u)
        set_tables(0)
        acc_g[...] = jnp.zeros_like(acc_g)
        acc_u[...] = jnp.zeros_like(acc_u)
        acc_h[...] = jnp.zeros_like(acc_h)

        @pl.when(inner)
        def _():
            for n in range(2):
                info_wait(n)
                set_tables(n + 1)

        def dispatch(u):
            which, i = split(u)
            gain_row = jnp.where(which == 0, gain_ref[:, cols_of(i)], 1.0)

            def slots(n, value):
                factor = jnp.where(which == 0, scale[n, 2], 1.0)
                return dot_nn(pick[n], (value.astype(F32) * factor * gain_row).astype(BF16)).astype(BF16)

            taken = slots(0, own[which, :, cols_of(i)])
            stage[which, i, 0] = taken[:capacity]
            nbuf[which, i, 0] = taken[capacity:]

            @pl.when(inner)
            def _():
                for n in range(2):
                    raw_wait(which, i, n)
                    passed = slots(n + 1, raw[which, i, n])
                    stage[which, i, n + 2] = passed[:capacity]
                    nbuf[which, i, n + 1] = passed[capacity:]
                nb_copy(which, i, 3).start()

            @pl.when(outer)
            def _():
                nb_copy(which, i, 1).start()

        def nb_wait(which, i):
            @pl.when(inner)
            def _():
                nb_copy(which, i, 1).wait_recv()

            @pl.when(outer)
            def _():
                nb_copy(which, i, 3).wait_recv()

        def tile_rows(which, i):
            return stage[which, i].reshape(rows, tile)

        @pl.loop(0, tiles + 1)
        def _(i):
            @pl.when(i < tiles)
            def _():
                for which in (0, 1):
                    far_copy(which, i).wait_recv()
                    cross_copy(which, i).start()

                @pl.when(i + FAR_AHEAD < tiles)
                def _():
                    for which in (0, 1):
                        far_copy(which, i + FAR_AHEAD).start()

                @pl.when((i + FAR_AHEAD >= tiles) & (i < tiles))
                def _():
                    for n in range(2):
                        d = 2 * (i - max(tiles - FAR_AHEAD, 0)) + n

                        @pl.when(d < min(DOWN_AHEAD, tiles))
                        def _():
                            far_copy(2, d).start()

            @pl.when(i == min(4, tiles - 1))
            def _():
                near_copy(2).start()

            @pl.when((i >= 1) & (i < tiles))
            def _():
                for n in range(2):
                    u = 2 * (i - 1) + n

                    @pl.when(u + AHEAD < units)
                    def _():
                        raw_start(u + AHEAD)

                    dispatch(u)

            @pl.when(i < tiles)
            def _():
                @pl.when(i == 0)
                def _():
                    near_copy(0).wait_recv()
                    near_copy(1).wait_recv()

                for which in (0, 1):
                    cross_copy(which, i).wait_recv()
                load((0, 1), i)

            @pl.when(i >= 1)
            def _():
                t = i - 1
                nb_wait(0, t)
                loaded((0, 1), t)
                slot = lax.rem(t, 2)
                block = tile_rows(0, t)
                for j in range(SLICES):
                    acc_g[:, piece(j)] += dot_nn(block, buf_g[slot, j])
                    acc_u[:, piece(j)] += dot_nn(block, buf_u[slot, j])

        for j in range(SLICES):
            gate_pre = acc_g[:, piece(j)]
            hid[:, piece(j)] = (gate_pre * jax.nn.sigmoid(gate_pre) * acc_u[:, piece(j)]).astype(BF16)
        near_copy(2).wait_recv()

        def ship(which, i, total):
            stage[which, i] = total.astype(BF16).reshape(experts, capacity, tile)

            @pl.when(inner)
            def _():
                ret_copy(which, i, 1).start()

            @pl.when(outer)
            def _():
                ret_copy(which, i, 3).start()

        def relay(u):
            which, i = split(u)
            ret_copy(which, i, 3).wait_recv()
            for n in range(2):
                value = scale[n + 1, 0] * dot_nn(back[n + 1, 0], stage[which, i, n + 2])
                value += scale[n + 1, 1] * dot_nn(back[n + 1, 1], rbuf[which, i, n + 1])
                raw[which, i, n] = value.astype(BF16)
                cmb_copy(which, i, n).start()

        def finish(u):
            which, i = split(u)
            cols = cols_of(i)

            @pl.when(outer)
            def _():
                ret_copy(which, i, 1).wait_recv()

            cmb_copy(which, i, 0).wait_recv()
            value = cbuf[which, i].astype(F32)
            value += scale[0, 0] * dot_nn(back[0, 0], stage[which, i, 0])
            value += scale[0, 1] * dot_nn(back[0, 1], rbuf[which, i, 0])

            @pl.when(which == 0)
            def _():
                obuf[0, i] = (own[0, :, cols].astype(F32) + value).astype(BF16)
                out_copy(0, i).start()

            @pl.when(which == 1)
            def _():
                @pl.when(i == 0)
                def _():
                    full = full_of(0)
                    total = jnp.zeros((token_count, 1), F32)
                    for n, expert in enumerate((mine, pair, opposite[0], opposite[1])):
                        if n > 0:
                            rho_wait(n)
                        found = lane_value == column(full, expert)
                        taken = jnp.sum(jnp.where(found, rho_in[n, 0:1], 0.0), axis=1, keepdims=True)
                        total += column(full, experts + expert) * taken
                    coef[...] = scale[0, 2] * scale[0, 2] * total / width

                grown = scale[0, 2] * (value * gain_ref[:, cols])
                obuf[1, i] = (
                    own[1, :, cols].astype(F32) + grown - own[0, :, cols].astype(F32) * coef[...]
                ).astype(BF16)
                out_copy(1, i).start()

        def returns(u):
            r = u - RELAY_LAG

            @pl.when((r >= 0) & (r < units) & inner)
            def _():
                relay(r)

            f = r - FINISH_LAG

            @pl.when((f >= 0) & (f < units))
            def _():
                finish(f)

        @pl.loop(0, tiles + 1)
        def _(i):
            @pl.when(i < tiles)
            def _():
                far_copy(2, i).wait_recv()
                cross_copy(2, i).start()

                @pl.when(i + DOWN_AHEAD < tiles)
                def _():
                    far_copy(2, i + DOWN_AHEAD).start()

            @pl.when(i >= 1)
            def _():
                t = i - 1
                loaded((2,), t)
                slot = lax.rem(t, 2)
                ship(0, t, dot_nn(hid[...], buf_d[slot].reshape(hidden, tile)))

            @pl.when(i < 2)
            def _():
                dispatch(units - 2 + i)

            @pl.when(i < tiles)
            def _():
                cross_copy(2, i).wait_recv()
                load((2,), i)

            @pl.when(i >= 1)
            def _():
                t = i - 1
                slot = lax.rem(t, 2)
                nb_wait(1, t)
                acc_h[...] += dot_nt(tile_rows(1, t), buf_d[slot].reshape(hidden, tile))

            returns(i - 1)

        load((0, 1), 0)
        rho = jnp.zeros((rows, 1), F32)
        for j in range(SLICES):
            gate_pre, up_pre, grad_hidden = acc_g[:, piece(j)], acc_u[:, piece(j)], acc_h[:, piece(j)]
            sig = jax.nn.sigmoid(gate_pre)
            grad_gate = (grad_hidden * up_pre * sig * (1.0 + gate_pre * (1.0 - sig))).astype(BF16)
            grad_up = (grad_hidden * (gate_pre * sig)).astype(BF16)
            gg[:, piece(j)] = grad_gate
            ug[:, piece(j)] = grad_up
            rho += jnp.sum(
                grad_gate.astype(F32) * gate_pre + grad_up.astype(F32) * up_pre, axis=1, keepdims=True
            )
        diagonal = lax.broadcasted_iota(jnp.int32, (capacity, LANES), 0) == lax.broadcasted_iota(
            jnp.int32, (capacity, LANES), 1
        )
        for n in range(experts):
            line = jnp.sum(
                jnp.where(diagonal, rho[n * capacity : (n + 1) * capacity], 0.0), axis=0, keepdims=True
            )
            target = rho_in if n == 0 else rho_out
            target[n] = jnp.broadcast_to(line, target.shape[1:])
        for copy in rho_copies():
            copy.start()

        @pl.loop(0, tiles + RELAY_LAG + FINISH_LAG)
        def _(i):
            @pl.when(i + 1 < tiles)
            def _():
                load((0, 1), i + 1)

            @pl.when(i < tiles)
            def _():
                loaded((0, 1), i)
                slot = lax.rem(i, 2)
                total = dot_nt(gg[:, piece(0)], buf_g[slot, 0]) + dot_nt(ug[:, piece(0)], buf_u[slot, 0])
                for j in range(1, SLICES):
                    total += dot_nt(gg[:, piece(j)], buf_g[slot, j]) + dot_nt(ug[:, piece(j)], buf_u[slot, j])
                ship(1, i, total)

            returns(tiles + i)

        def sent(block, sem):
            remote(block, block, sem, rho_r.at[0], device_of(pair)).wait_send()

        for which in range(3):
            weight, full, _ = weights[which]
            sent(weight, far_s.at[which])
            sent(full.at[1], cross_s.at[which])
            sent(weight, near_s.at[which])
        sent(own, raw_s)
        sent(info.at[0], info_s)
        for copy in rho_copies():
            copy.wait_send()

        @pl.when(inner)
        def _():
            sent(nbuf, nb_s)
            sent(stage.at[:, :, pl.ds(1, 1)], ret_s)
            sent(raw, cmb_s)

        @pl.when(outer)
        def _():
            sent(nbuf.at[:, :, pl.ds(0, 1)], nb_s)
            sent(stage.at[:, :, pl.ds(1, 3)], ret_s)

        for which, ref in enumerate((next_ref, prev_ref)):
            sent(obuf.at[which], out_s.at[which])
            remote(ref, ref, out_s.at[which], out_r.at[which], (after, me)).wait_recv()

    three = lambda value: jax.ShapeDtypeStruct((3,) + value.shape, value.dtype)
    in_vmem = pl.BlockSpec(memory_space=pltpu.VMEM)
    result = jax.ShapeDtypeStruct((token_count, width), BF16)
    dma = pltpu.SemaphoreType.DMA
    vmem = pltpu.VMEM
    wide = (rows, hidden)
    return pl.pallas_call(
        kernel,
        in_specs=[in_vmem] * 2 + [ANY] * 5,
        out_specs=[ANY] * 5,
        out_shape=[result] * 2 + [three(gate), three(up), three(down)],
        scratch_shapes=[
            vmem((2, token_count, width), BF16),
            vmem((2, tiles, experts, capacity, tile), BF16),
            vmem((2, tiles, 3, capacity, tile), BF16),
            vmem((2, tiles, 3, capacity, tile), BF16),
            vmem((2, tiles, 2, token_count, tile), BF16),
            vmem((2, tiles, token_count, tile), BF16),
            vmem((2, tiles, token_count, tile), BF16),
            vmem((3, 16, LANES), F32),
            vmem((LANES, LANES), F32),
            vmem((3, 2 * capacity, token_count), BF16),
            vmem((3, 2, token_count, capacity), BF16),
            vmem((3, 3, token_count, 1), F32),
            vmem((token_count, 1), F32),
            vmem((4, 8, LANES), F32),
            vmem((4, 8, LANES), F32),
        ]
        + [vmem(wide, F32)] * 3
        + [vmem(wide, BF16)] * 3
        + [vmem((2, SLICES, tile, ffd), BF16)] * 2
        + [vmem((2, SLICES, ffd, tile), BF16)]
        + [
            dma((2,)), dma, dma((2, tiles, 2)), dma, dma((2,)),
            dma, dma((2, tiles)), dma, dma((2, tiles)), dma, dma((2, tiles)),
            dma((3,)), dma((4,)), dma((2,)), dma((2,)),
            dma((3,)), dma((3, tiles)), dma((3,)), dma((3, tiles)), dma((3,)), dma((3,)),
            dma((3, 2, SLICES)),
        ],
        compiler_params=pltpu.CompilerParams(
            collective_id=1, has_side_effects=True, vmem_limit_bytes=VMEM
        ),
        name="relay_layer",
    )(table, gain, gate, up, down, tokens, grad_rows)[:2]


def slots_of(route_ids, home, experts, capacity):
    token_count, top_count = route_ids.shape
    relative = (route_ids.reshape(-1) - home + experts) % experts
    onehot = (relative[:, None] == jnp.arange(experts, dtype=jnp.int32)[None, :]).astype(jnp.int32)
    order = jnp.arange(onehot.shape[0], dtype=jnp.int32)
    earlier = (order[:, None] > order[None, :]).astype(BF16)
    before = dot_nn(earlier, onehot.astype(BF16)).astype(jnp.int32)
    target = relative * capacity + jnp.sum(before * onehot, axis=1)
    return target.reshape(token_count, top_count)


def pickers_of(pair_slot, experts, capacity):
    flat = pair_slot.T.reshape(-1)
    slots = jnp.arange(experts * capacity, dtype=jnp.int32).reshape(experts, 1, capacity)
    return (flat[None, :, None] == slots).astype(BF16)


def inverse_of(values):
    return lax.rsqrt(jnp.mean(values * values, axis=-1, keepdims=True) + EPSILON)


def body(tokens, grad_out, norm_gain, expert_ids, gate_weights, w_gate, w_up, w_down):
    tokens = tokens[0]
    grad_rows = grad_out[0]
    gain = norm_gain[0][None, :]
    route_ids = expert_ids[0]
    route_weights = gate_weights[0]
    token_count, width = tokens.shape
    top_count = route_ids.shape[1]
    devices = lax.axis_size("expert")
    pipes = lax.axis_size("pipe")
    experts = devices // SLICES
    step_size = 4 * experts * SLICES
    capacity = min(
        token_count, SLICES * ((token_count * top_count * 5 + step_size - 1) // step_size)
    )
    home = lax.axis_index("expert") // SLICES
    same = lambda d: d

    gate, up, down = w_gate[0], w_up[0], w_down[0]

    if experts == 4 and token_count == LANES:
        table = jnp.concatenate(
            [route_ids.astype(F32), route_weights, jnp.zeros((token_count, LANES - 2 * top_count), F32)], axis=1
        )
        next_rows, prev_rows = relay_layer(
            table, gain, gate, up, down, tokens, grad_rows, capacity, top_count
        )
        return (next_rows[None], prev_rows[None])

    values = tokens.astype(F32)
    inverse = inverse_of(values)
    pair_slot = slots_of(route_ids, home, experts, capacity)
    picker = jnp.any(
        pair_slot[None, :, :]
        == jnp.arange(experts * capacity, dtype=jnp.int32)[:, None, None],
        axis=2,
    ).astype(BF16)

    routing = jnp.concatenate([pair_slot.astype(F32), route_weights, inverse], axis=1)
    routing_next = move(routing, 1, same)
    routing_prev = routing_next if pipes == 2 else move(routing, -1, same)
    gain_prev = move(gain, -1, same)

    def routing_of(table):
        slots = table[:, :top_count].astype(jnp.int32)
        return pickers_of(slots, experts, capacity), table[:, top_count : 2 * top_count]

    pick_next, weights_next = routing_of(routing_next)
    pick_prev, weights_prev = routing_of(routing_prev)
    next_rows, prev_rows = layer(
        picker, inverse, gain, gate, up, down, tokens, grad_rows,
        gain_prev, routing_prev[:, 2 * top_count :],
        pick_next, weights_next, pick_prev, weights_prev,
    )
    return (next_rows[None], prev_rows[None])


def solution(mesh):
    return jax.shard_map(
        body,
        mesh=mesh,
        in_specs=(
            P("pipe", "expert", None),
            P("pipe", "expert", None),
            P("pipe", None),
            P("pipe", "expert", None),
            P("pipe", "expert", None),
            P("pipe", None, "expert"),
            P("pipe", None, "expert"),
            P("pipe", "expert", None),
        ),
        out_specs=(P("pipe", "expert", None), P("pipe", "expert", None)),
        check_vma=False,
    )
```

```python
import jax
import jax.numpy as jnp
from jax import lax
from jax.experimental import pallas as pl
from jax.experimental.pallas import tpu as pltpu
from jax.sharding import PartitionSpec as P

SLICES = 4
EPSILON = 1e-06
BF16 = jnp.bfloat16
F32 = jnp.float32


def move(value, pipe_steps, expert_map):
    pipes, devices = lax.axis_size("pipe"), lax.axis_size("expert")
    pairs = [
        (p * devices + d, ((p + pipe_steps) % pipes) * devices + expert_map(d))
        for p in range(pipes)
        for d in range(devices)
    ]
    return lax.ppermute(value, ("pipe", "expert"), pairs)


def dot_nt(left_arr, right_arr):
    return lax.dot_general(
        left_arr, right_arr, (((1,), (1,)), ((), ())), preferred_element_type=F32
    )


def dot_nn(left_arr, right_arr):
    return jnp.dot(left_arr, right_arr, preferred_element_type=F32)


def tile_of(width):
    for tile in (1024, 512, 256, 128):
        if width % tile == 0:
            return tile
    return width


MESH = pl.DeviceIdType.MESH
ANY = pl.BlockSpec(memory_space=pl.ANY)


def sections():
    pipe, pipes = lax.axis_index("pipe"), lax.axis_size("pipe")
    return pipe, lax.rem(pipe + 1, pipes), lax.rem(pipe + pipes - 1, pipes)


def greet(partners):
    barrier = pltpu.get_barrier_semaphore()
    for partner in partners:
        pl.semaphore_signal(barrier, inc=1, device_id=partner, device_id_type=MESH)
    pl.semaphore_wait(barrier, len(partners))


VMEM = 62 * 1024 * 1024


def layer(picker, inverse, gain, gate, up, down, tokens, grad_rows,
          gain_prev, inverse_prev, pick_next, wt_next, pick_prev, wt_prev):
    rows = picker.shape[0]
    experts, _, capacity = pick_next.shape
    width = tokens.shape[1]
    ffd = down.shape[0]
    token_count, top = wt_next.shape
    devices, pipes = lax.axis_size("expert"), lax.axis_size("pipe")
    tile = tile_of(width)
    tiles = width // tile

    def kernel(pick, inv_own, gain_own, wg, wu, wd, tok, grd, gain, inv, pn, wn, pp, wp,
               next_ref, prev_ref, ag, au, ad,
               ri, rg, si, sg, tn, tp, gp, recv_o, recv_g, scaled, acc_g, acc_u, acc_h, hid, gg, ug,
               buf_g, buf_u, buf_d,
               far_s, far_r, cross_s, cross_r, near_s, near_r, rows_s, rows_r, tok_s, tok_r,
               load_sem, send, recv):
        pipe, after, ahead = sections()
        me = lax.axis_index("expert")
        place = lax.rem(me, SLICES)
        far = me - place + lax.rem(place + 2, SLICES)
        near = me + 1 - 2 * lax.rem(me, 2)
        others = [lax.rem(me + SLICES * s, devices) for s in range(1, experts)]
        homes = [lax.rem(me + devices - SLICES * s, devices) for s in range(experts)]
        greet(
            [(pipe, d) for d in others]
            + [(pipe, far), (pipe, near)]
            + [(p, d) for p in (after, ahead) for d in homes]
        )
        weights = ((wg, ag, buf_g), (wu, au, buf_u), (wd, ad, buf_d))
        stages = (ri, rg)

        def remote(source, target, send_sem, recv_sem, device):
            return pltpu.make_async_remote_copy(
                src_ref=source, dst_ref=target, send_sem=send_sem, recv_sem=recv_sem,
                device_id=device, device_id_type=MESH,
            )

        def cols_of(i):
            return pl.ds(pl.multiple_of(i * tile, tile), tile)

        def part(ref, which, i):
            return ref.at[cols_of(i), :] if which < 2 else ref.at[:, cols_of(i)]

        def far_copy(which, i):
            own, full, _ = weights[which]
            return remote(
                part(own, which, i), part(full.at[1], which, i),
                far_s.at[which, i], far_r.at[which, i], (pipe, far),
            )

        def cross_copy(which, i):
            full = weights[which][1]
            return remote(
                part(full.at[1], which, i), part(full.at[2], which, i),
                cross_s.at[which, i], cross_r.at[which, i], (pipe, near),
            )

        def near_copy(which):
            own, full, _ = weights[which]
            return remote(own, full.at[0], near_s.at[which], near_r.at[which], (pipe, near))

        def row_copy(which, i, s):
            return remote(
                (si, sg)[which].at[s - 1, :, cols_of(i)], stages[which].at[s, :, cols_of(i)],
                rows_s.at[which, i, s - 1], rows_r.at[which, i, s - 1], (pipe, others[s - 1]),
            )

        def token_copies():
            moves = [(tok, tn, after), (grd, gp, ahead), (tok, tp, ahead)]
            return [
                remote(source, target, tok_s.at[n], tok_r.at[n], (device, me))
                for n, (source, target, device) in enumerate(moves)
            ]

        def loads(which, i):
            own, full, buf = weights[which]
            slot = lax.rem(i, 2)
            return [
                pltpu.make_async_copy(
                    part(own if j == 0 else full.at[j - 1], which, i),
                    buf.at[slot, j],
                    load_sem.at[which, slot, j],
                )
                for j in range(SLICES)
            ]

        def load(kinds, i):
            for which in kinds:
                for copy in loads(which, i):
                    copy.start()

        def loaded(kinds, i):
            for which in kinds:
                for copy in loads(which, i):
                    copy.wait()

        def result_copy(which, i, s):
            return remote(
                stages[which].at[s, :, cols_of(i)], (recv_o, recv_g)[which].at[s, :, cols_of(i)],
                send.at[which, i, s], recv.at[which, i, s], ((after, ahead)[which], homes[s]),
            )

        def ship(which, i, total):
            for s in range(experts):
                stages[which][s, :, cols_of(i)] = total[s * capacity : (s + 1) * capacity].astype(BF16)
            for s in range(experts):
                result_copy(which, i, s).start()

        def send_rows(which, i):
            cols = cols_of(i)
            value = tok[:, cols].astype(F32) * inv_own[...] * gain_own[:, cols] if which == 0 else grd[:, cols]
            slots = dot_nn(pick[...], value.astype(BF16))
            stages[which][0, :, cols] = slots[:capacity].astype(BF16)
            for s in range(1, experts):
                (si, sg)[which][s - 1, :, cols] = slots[s * capacity : (s + 1) * capacity].astype(BF16)
            for s in range(experts - 1, 0, -1):
                row_copy(which, i, s).start()

        def send_far(kinds, i):
            for which in kinds:
                far_copy(which, i).start()

        def tile_rows(which, i):
            return stages[which][:, :, cols_of(i)].reshape(rows, tile)

        def piece(j):
            return slice(j * ffd, (j + 1) * ffd)

        first_far, first_down = min(2, tiles), min(4, tiles)
        for i in range(first_far):
            send_far((0, 1), i)

        @pl.loop(0, tiles)
        def _(i):
            send_rows(0, i)

        for which in range(3):
            near_copy(which).start()
        for copy in token_copies():
            copy.start()
        acc_g[...] = jnp.zeros_like(acc_g)
        acc_u[...] = jnp.zeros_like(acc_u)
        acc_h[...] = jnp.zeros_like(acc_h)
        near_copy(0).wait()
        near_copy(1).wait()

        def pipeline(kinds, arrive, compute):
            @pl.loop(0, tiles + 2)
            def _(i):
                @pl.when(i < tiles)
                def _():
                    arrive(i)
                    for which in kinds:
                        far_copy(which, i).wait()
                        cross_copy(which, i).start()

                @pl.when((i >= 1) & (i <= tiles))
                def _():
                    for which in kinds:
                        cross_copy(which, i - 1).wait()
                    load(kinds, i - 1)

                @pl.when(i >= 2)
                def _():
                    loaded(kinds, i - 2)
                    compute(i - 2)

        def arrive_first(i):
            send_rows(1, i)

            @pl.when(i + first_far < tiles)
            def _():
                send_far((0, 1), i + first_far)

            @pl.when(i == tiles - 1)
            def _():
                for n in range(first_down):
                    send_far((2,), n)

        def compute_first(i):
            for s in range(1, experts):
                row_copy(0, i, s).wait()
            slot = lax.rem(i, 2)
            block = tile_rows(0, i)
            for j in range(SLICES):
                acc_g[:, piece(j)] += dot_nn(block, buf_g[slot, j])
                acc_u[:, piece(j)] += dot_nn(block, buf_u[slot, j])

        pipeline((0, 1), arrive_first, compute_first)

        for j in range(SLICES):
            gate_pre = acc_g[:, piece(j)]
            hid[:, piece(j)] = (gate_pre * jax.nn.sigmoid(gate_pre) * acc_u[:, piece(j)]).astype(BF16)
        near_copy(2).wait()

        def arrive_down(i):
            @pl.when(i + first_down < tiles)
            def _():
                send_far((2,), i + first_down)

        def compute_down(i):
            slot = lax.rem(i, 2)
            total = dot_nn(hid[:, piece(0)], buf_d[slot, 0])
            for j in range(1, SLICES):
                total += dot_nn(hid[:, piece(j)], buf_d[slot, j])
            ship(0, i, total)
            for s in range(1, experts):
                row_copy(1, i, s).wait()
            block = tile_rows(1, i)
            for j in range(SLICES):
                acc_h[:, piece(j)] += dot_nt(block, buf_d[slot, j])

        pipeline((2,), arrive_down, compute_down)

        load((0, 1), 0)
        for j in range(SLICES):
            gate_pre, up_pre, grad_hidden = acc_g[:, piece(j)], acc_u[:, piece(j)], acc_h[:, piece(j)]
            sig = jax.nn.sigmoid(gate_pre)
            gg[:, piece(j)] = (grad_hidden * up_pre * sig * (1.0 + gate_pre * (1.0 - sig))).astype(BF16)
            ug[:, piece(j)] = (grad_hidden * (gate_pre * sig)).astype(BF16)

        @pl.loop(0, tiles)
        def _(i):
            @pl.when(i + 1 < tiles)
            def _():
                load((0, 1), i + 1)

            loaded((0, 1), i)
            slot = lax.rem(i, 2)
            total = dot_nt(gg[:, piece(0)], buf_g[slot, 0]) + dot_nt(ug[:, piece(0)], buf_u[slot, 0])
            for j in range(1, SLICES):
                total += dot_nt(gg[:, piece(j)], buf_g[slot, j]) + dot_nt(ug[:, piece(j)], buf_u[slot, j])
            ship(1, i, total)

        def picked(target, pick, scale, cols):
            total = dot_nn(pick[0], target[0, :, cols])
            for s in range(1, experts):
                total += dot_nn(pick[s], target[s, :, cols])
            value = total[:token_count] * scale[:, 0:1]
            for n in range(1, top):
                value += total[n * token_count : (n + 1) * token_count] * scale[:, n : n + 1]
            return value

        for copy in token_copies():
            copy.wait()

        @pl.loop(0, tiles)
        def _(i):
            cols = cols_of(i)
            for s in range(experts):
                result_copy(0, i, s).wait()
            next_ref[:, cols] = (tn[:, cols].astype(F32) + picked(recv_o, pn, wn, cols)).astype(BF16)

        def finish(i, mean):
            cols = cols_of(i)
            for s in range(experts):
                result_copy(1, i, s).wait()
            value = picked(recv_g, pp, wp, cols) * gain[:, cols]
            scaled[:, cols] = value
            return mean + jnp.sum(value * tp[:, cols].astype(F32), axis=1, keepdims=True)

        mean = lax.fori_loop(0, tiles, finish, jnp.zeros((token_count, 1), F32)) / width
        inverse = inv[...]
        factor = inverse * inverse * inverse * mean

        @pl.loop(0, tiles)
        def _(i):
            cols = cols_of(i)
            prev_ref[:, cols] = (
                gp[:, cols].astype(F32) + inverse * scaled[:, cols] - tp[:, cols].astype(F32) * factor
            ).astype(BF16)

    three = lambda value: jax.ShapeDtypeStruct((3,) + value.shape, value.dtype)
    in_vmem = pl.BlockSpec(memory_space=pltpu.VMEM)
    result = jax.ShapeDtypeStruct((token_count, width), BF16)
    row_block = pltpu.VMEM((experts, capacity, width), BF16)
    token_block = pltpu.VMEM((token_count, width), BF16)
    wide = (rows, SLICES * ffd)
    dma = pltpu.SemaphoreType.DMA
    return pl.pallas_call(
        kernel,
        in_specs=[in_vmem] * 3 + [ANY] * 3 + [in_vmem] * 8,
        out_specs=[in_vmem] * 2 + [ANY] * 3,
        out_shape=[result] * 2 + [three(gate), three(up), three(down)],
        scratch_shapes=[row_block] * 2
        + [pltpu.VMEM((experts - 1, capacity, width), BF16)] * 2
        + [token_block] * 3
        + [row_block] * 2
        + [pltpu.VMEM((token_count, width), F32)]
        + [pltpu.VMEM(wide, F32)] * 3
        + [pltpu.VMEM(wide, BF16)] * 3
        + [pltpu.VMEM((2, SLICES, tile, ffd), BF16)] * 2
        + [pltpu.VMEM((2, SLICES, ffd, tile), BF16)]
        + [dma((3, tiles))] * 4
        + [dma((3,))] * 2
        + [dma((2, tiles, experts - 1))] * 2
        + [dma((3,))] * 2
        + [dma((3, 2, SLICES))]
        + [dma((2, tiles, experts))] * 2,
        compiler_params=pltpu.CompilerParams(
            collective_id=0, has_side_effects=True, vmem_limit_bytes=VMEM
        ),
        name="layer",
    )(picker, inverse, gain, gate, up, down, tokens, grad_rows,
      gain_prev, inverse_prev, pick_next, wt_next, pick_prev, wt_prev)[:2]


LANES = 128
TILE = 256
AHEAD = 8
FAR_AHEAD = 4
DOWN_AHEAD = 8
FINISH_LAG = 6


def relay_layer(ids, shares, gain, gate, up, down, tokens, grad_rows, capacity, top):
    experts = 4
    token_count, width = tokens.shape
    ffd = down.shape[0]
    hidden = SLICES * ffd
    rows = experts * capacity
    devices = lax.axis_size("expert")
    tile = min(TILE, tile_of(width))
    tiles = width // tile
    units = 2 * tiles

    def kernel(ids_ref, shares_ref, gain_ref, wg, wu, wd, tok, grd,
               next_ref, prev_ref, ag, au, ad,
               own, stage, nbuf, rbuf, raw, cbuf, obuf, info, square, pick, back, scale, coef,
               rho_out, rho_in, acc_g, acc_u, acc_h, hid, gg, ug, buf_g, buf_u, buf_d,
               own_l, raw_s, raw_r, info_s, info_r, nb_s, nb_r, ret_s, ret_r, cmb_s, cmb_r,
               rho_s, rho_r, out_s, out_r, far_s, far_r, cross_s, cross_r, near_s, near_r, load_sem):
        pipe, after, ahead = sections()
        me = lax.axis_index("expert")
        place = lax.rem(me, SLICES)
        mine = lax.div(me, SLICES)
        half = lax.div(mine, 2)
        outer_index = 1 - lax.rem(lax.div(mine + 1, 2), 2)
        inner = outer_index == 0
        outer = outer_index == 1
        far = me - place + lax.rem(place + 2, SLICES)
        near = me + 1 - 2 * lax.rem(me, 2)

        def device_of(expert):
            return (pipe, expert * SLICES + place)

        pair = mine + 1 - 2 * lax.rem(mine, 2)
        opposite = [2 - half, 3 - 3 * half]
        greet(
            [(pipe, lax.rem(me + SLICES * s, devices)) for s in range(1, experts)]
            + [(pipe, far), (pipe, near), (after, me), (ahead, me)]
        )
        weights = ((wg, ag, buf_g), (wu, au, buf_u), (wd, ad, buf_d))

        def remote(source, target, send_sem, recv_sem, device):
            return pltpu.make_async_remote_copy(
                src_ref=source, dst_ref=target, send_sem=send_sem, recv_sem=recv_sem,
                device_id=device, device_id_type=MESH,
            )

        def cols_of(i):
            return pl.ds(pl.multiple_of(i * tile, tile), tile)

        def part(ref, which, i):
            return ref.at[cols_of(i), :] if which < 2 else ref.at[:, cols_of(i)]

        def far_copy(which, i):
            weight, full, _ = weights[which]
            return remote(
                part(weight, which, i), part(full.at[1], which, i),
                far_s.at[which], far_r.at[which, i], (pipe, far),
            )

        def cross_copy(which, i):
            full = weights[which][1]
            return remote(
                part(full.at[1], which, i), part(full.at[2], which, i),
                cross_s.at[which], cross_r.at[which, i], (pipe, near),
            )

        def near_copy(which):
            weight, full, _ = weights[which]
            return remote(weight, full.at[0], near_s.at[which], near_r.at[which], (pipe, near))

        def loads(which, i):
            weight, full, buf = weights[which]
            slot = lax.rem(i, 2)
            cols = cols_of(i)
            gathered = full.at[:, cols, :] if which < 2 else full.at[:, :, cols]
            return [
                pltpu.make_async_copy(part(weight, which, i), buf.at[slot, 0], load_sem.at[which, slot, 0]),
                pltpu.make_async_copy(gathered, buf.at[slot, pl.ds(1, SLICES - 1)], load_sem.at[which, slot, 1]),
            ]

        def load(kinds, i):
            for which in kinds:
                for copy in loads(which, i):
                    copy.start()

        def loaded(kinds, i):
            for which in kinds:
                for copy in loads(which, i):
                    copy.wait()

        def split(u):
            return lax.div(u, tiles), lax.rem(u, tiles)

        def raw_copy(source, which, i):
            return remote(
                source, raw.at[which, i, outer_index], raw_s, raw_r.at[which, i, outer_index],
                device_of(opposite[0]),
            )

        def raw_start(u):
            which, i = split(u)
            raw_copy(own.at[which, :, cols_of(i)], which, i).start()

        def raw_wait(which, i, n):
            block = raw.at[which, i, n]
            remote(block, block, raw_s, raw_r.at[which, i, n], device_of(opposite[0])).wait_recv()

        def info_copy():
            return remote(
                info.at[0], info.at[1 + outer_index], info_s, info_r.at[outer_index], device_of(opposite[0])
            )

        def info_wait(n):
            block = info.at[1 + n]
            remote(block, block, info_s, info_r.at[n], device_of(opposite[0])).wait_recv()

        def nb_copy(which, i, blocks):
            return remote(
                nbuf.at[which, i, pl.ds(0, blocks)], stage.at[which, i, pl.ds(1, blocks)],
                nb_s, nb_r.at[which, i], device_of(pair),
            )

        def ret_copy(which, i, blocks):
            return remote(
                stage.at[which, i, pl.ds(1, blocks)], rbuf.at[which, i, pl.ds(0, blocks)],
                ret_s, ret_r.at[which, i], device_of(pair),
            )

        def cmb_copy(which, i, n):
            return remote(
                raw.at[which, i, n], cbuf.at[which, i], cmb_s, cmb_r.at[which, i], device_of(opposite[n])
            )

        def out_copy(which, i):
            return remote(
                obuf.at[which, i], (next_ref, prev_ref)[which].at[:, cols_of(i)],
                out_s.at[which], out_r.at[which], ((after, ahead)[which], me),
            )

        def rho_copies():
            places = (1, 2 + outer_index, 2 + outer_index)
            targets = (pair, opposite[0], opposite[1])
            return [
                remote(rho_out.at[n + 1], rho_in.at[places[n]], rho_s.at[n], rho_r.at[places[n]], device_of(targets[n]))
                for n in range(3)
            ]

        def rho_wait(n):
            block = rho_in.at[n]
            remote(block, block, rho_s.at[0], rho_r.at[n], device_of(pair)).wait_recv()

        own_loads = [
            pltpu.make_async_copy(source, own.at[n], own_l.at[n]) for n, source in enumerate((tok, grd))
        ]

        def piece(j):
            return slice(j * ffd, (j + 1) * ffd)

        for copy in own_loads:
            copy.start()
        first_raw = min(2, tiles)
        for i in range(min(FAR_AHEAD, tiles)):
            for which in (0, 1):
                far_copy(which, i).start()
            if i < first_raw:
                raw_copy(tok.at[:, cols_of(i)], 0, i).start()
        near_copy(0).start()
        near_copy(1).start()

        lane = lax.broadcasted_iota(jnp.int32, (token_count, LANES), 1)
        lane_value = lane.astype(F32)

        def full_of(n):
            square[...] = jnp.zeros_like(square)
            square[: info.shape[1]] = info[n]
            return square[...].T

        def column(full, index):
            return jnp.sum(jnp.where(lane == index, full, 0.0), axis=1, keepdims=True)

        def set_tables(n):
            full = full_of(n)
            slot = lax.broadcasted_iota(jnp.int32, (capacity, token_count), 0).astype(F32)
            slot_lane = lax.broadcasted_iota(jnp.int32, (token_count, capacity), 1).astype(F32)
            for k, expert in enumerate((mine, pair)):
                pick[n, k * capacity : (k + 1) * capacity] = (slot == info[n, pl.ds(expert, 1), :]).astype(BF16)
                back[n, k] = (slot_lane == column(full, expert)).astype(BF16)
                scale[n, k] = column(full, experts + expert)
            scale[n, 2] = column(full, 2 * experts)

        own_loads[0].wait()

        def add_squares(i, total):
            value = own[0, :, cols_of(i)].astype(F32)
            return total + jnp.sum(value * value, axis=1, keepdims=True)

        squares = lax.fori_loop(0, tiles, add_squares, jnp.zeros((token_count, 1), F32))
        inverse_own = lax.rsqrt(squares / width + EPSILON)
        expert_row = lax.broadcasted_iota(jnp.int32, (8, LANES), 0)
        hit = jnp.zeros((8, LANES), F32)
        weight_of = jnp.zeros((8, LANES), F32)
        for k in range(top):
            named = expert_row == ids_ref[k : k + 1]
            hit += jnp.where(named, 1.0, 0.0)
            weight_of += jnp.where(named, shares_ref[k : k + 1], 0.0)
        earlier = (lax.broadcasted_iota(jnp.int32, (token_count, LANES), 0) < lane).astype(BF16)
        before = dot_nn(hit.astype(BF16), earlier)
        square[...] = jnp.zeros_like(square)
        square[:experts] = jnp.where(hit > 0.5, before, -1.0)[:experts]
        square[experts : 2 * experts] = weight_of[:experts]
        full_own = jnp.where(lane == 2 * experts, inverse_own, square[...].T)
        info[0] = full_own.T[: info.shape[1]]
        info_copy().start()
        own_loads[1].wait()
        for u in range(first_raw, min(AHEAD, units)):
            raw_start(u)
        set_tables(0)
        acc_g[...] = jnp.zeros_like(acc_g)
        acc_u[...] = jnp.zeros_like(acc_u)
        acc_h[...] = jnp.zeros_like(acc_h)

        @pl.when(inner)
        def _():
            for n in range(2):
                info_wait(n)
                set_tables(n + 1)

        def dispatch(u):
            which, i = split(u)
            gain_row = jnp.where(which == 0, gain_ref[:, cols_of(i)], 1.0)

            def slots(n, value):
                factor = jnp.where(which == 0, scale[n, 2], 1.0)
                return dot_nn(pick[n], (value.astype(F32) * factor * gain_row).astype(BF16)).astype(BF16)

            taken = slots(0, own[which, :, cols_of(i)])
            stage[which, i, 0] = taken[:capacity]
            nbuf[which, i, 0] = taken[capacity:]

            @pl.when(inner)
            def _():
                for n in range(2):
                    raw_wait(which, i, n)
                    passed = slots(n + 1, raw[which, i, n])
                    stage[which, i, n + 2] = passed[:capacity]
                    nbuf[which, i, n + 1] = passed[capacity:]
                nb_copy(which, i, 3).start()

            @pl.when(outer)
            def _():
                nb_copy(which, i, 1).start()

        def nb_wait(which, i):
            @pl.when(inner)
            def _():
                nb_copy(which, i, 1).wait_recv()

            @pl.when(outer)
            def _():
                nb_copy(which, i, 3).wait_recv()

        def tile_rows(which, i):
            return stage[which, i].reshape(rows, tile)

        @pl.loop(0, tiles + 1)
        def _(i):
            @pl.when((i >= 1) & (i < tiles))
            def _():
                for n in range(2):
                    u = 2 * (i - 1) + n

                    @pl.when(u + AHEAD < units)
                    def _():
                        raw_start(u + AHEAD)

                    dispatch(u)

            @pl.when(i >= 1)
            def _():
                t = i - 1
                nb_wait(0, t)
                loaded((0, 1), t)
                slot = lax.rem(t, 2)
                block = tile_rows(0, t)
                for j in range(SLICES):
                    acc_g[:, piece(j)] += dot_nn(block, buf_g[slot, j])
                    acc_u[:, piece(j)] += dot_nn(block, buf_u[slot, j])

            @pl.when(i < tiles)
            def _():
                for which in (0, 1):
                    far_copy(which, i).wait_recv()
                    cross_copy(which, i).start()

                @pl.when(i + FAR_AHEAD < tiles)
                def _():
                    for which in (0, 1):
                        far_copy(which, i + FAR_AHEAD).start()

                @pl.when(i + FAR_AHEAD >= tiles)
                def _():
                    for n in range(2):
                        d = 2 * (i - max(tiles - FAR_AHEAD, 0)) + n

                        @pl.when(d < min(DOWN_AHEAD, tiles))
                        def _():
                            far_copy(2, d).start()

                @pl.when(i == min(4, tiles - 1))
                def _():
                    near_copy(2).start()

                @pl.when(i == 0)
                def _():
                    near_copy(0).wait_recv()
                    near_copy(1).wait_recv()

                for which in (0, 1):
                    cross_copy(which, i).wait_recv()
                load((0, 1), i)

        near_copy(2).wait_recv()
        far_copy(2, 0).wait_recv()
        cross_copy(2, 0).start()
        for j in range(SLICES):
            gate_pre = acc_g[:, piece(j)]
            hid[:, piece(j)] = (gate_pre * jax.nn.sigmoid(gate_pre) * acc_u[:, piece(j)]).astype(BF16)

        def ship(which, i, total):
            stage[which, i] = total.astype(BF16).reshape(experts, capacity, tile)

            @pl.when(inner)
            def _():
                ret_copy(which, i, 1).start()

            @pl.when(outer)
            def _():
                ret_copy(which, i, 3).start()

        def relay(u):
            which, i = split(u)
            ret_copy(which, i, 3).wait_recv()
            for n in range(2):
                value = scale[n + 1, 0] * dot_nn(back[n + 1, 0], stage[which, i, n + 2])
                value += scale[n + 1, 1] * dot_nn(back[n + 1, 1], rbuf[which, i, n + 1])
                raw[which, i, n] = value.astype(BF16)
                cmb_copy(which, i, n).start()

        def finish(u):
            which, i = split(u)
            cols = cols_of(i)

            @pl.when(outer)
            def _():
                ret_copy(which, i, 1).wait_recv()

            cmb_copy(which, i, 0).wait_recv()
            value = cbuf[which, i].astype(F32)
            value += scale[0, 0] * dot_nn(back[0, 0], stage[which, i, 0])
            value += scale[0, 1] * dot_nn(back[0, 1], rbuf[which, i, 0])

            @pl.when(which == 0)
            def _():
                obuf[0, i] = (own[0, :, cols].astype(F32) + value).astype(BF16)
                out_copy(0, i).start()

            @pl.when(which == 1)
            def _():
                @pl.when(i == 0)
                def _():
                    full = full_of(0)
                    total = jnp.zeros((token_count, 1), F32)
                    for n, expert in enumerate((mine, pair, opposite[0], opposite[1])):
                        if n > 0:
                            rho_wait(n)
                        found = lane_value == column(full, expert)
                        taken = jnp.sum(jnp.where(found, rho_in[n, 0:1], 0.0), axis=1, keepdims=True)
                        total += column(full, experts + expert) * taken
                    coef[...] = scale[0, 2] * scale[0, 2] * total / width

                grown = scale[0, 2] * (value * gain_ref[:, cols])
                obuf[1, i] = (
                    own[1, :, cols].astype(F32) + grown - own[0, :, cols].astype(F32) * coef[...]
                ).astype(BF16)
                out_copy(1, i).start()

        def relay_at(u):
            @pl.when((u >= 0) & inner)
            def _():
                relay(u)

        def finish_at(u):
            @pl.when((u >= 0) & (u < units))
            def _():
                finish(u)

        cross_copy(2, 0).wait_recv()
        load((2,), 0)

        @pl.loop(0, tiles)
        def _(i):
            slot = lax.rem(i, 2)
            loaded((2,), i)
            ship(0, i, dot_nn(hid[...], buf_d[slot].reshape(hidden, tile)))

            @pl.when(i + 1 < tiles)
            def _():
                far_copy(2, i + 1).wait_recv()
                cross_copy(2, i + 1).start()

                @pl.when(i + DOWN_AHEAD < tiles)
                def _():
                    far_copy(2, i + DOWN_AHEAD).start()

            nb_wait(1, i)
            acc_h[...] += dot_nt(tile_rows(1, i), buf_d[slot].reshape(hidden, tile))

            @pl.when(i + 1 < tiles)
            def _():
                cross_copy(2, i + 1).wait_recv()
                load((2,), i + 1)

            @pl.when(i < 2)
            def _():
                dispatch(units - 2 + i)

            relay_at(i - 1)
            finish_at(i - 1 - FINISH_LAG)

        load((0, 1), 0)
        rho = jnp.zeros((rows, 1), F32)
        for j in range(SLICES):
            gate_pre, up_pre, grad_hidden = acc_g[:, piece(j)], acc_u[:, piece(j)], acc_h[:, piece(j)]
            sig = jax.nn.sigmoid(gate_pre)
            grad_gate = (grad_hidden * up_pre * sig * (1.0 + gate_pre * (1.0 - sig))).astype(BF16)
            grad_up = (grad_hidden * (gate_pre * sig)).astype(BF16)
            gg[:, piece(j)] = grad_gate
            ug[:, piece(j)] = grad_up
            rho += jnp.sum(
                grad_gate.astype(F32) * gate_pre + grad_up.astype(F32) * up_pre, axis=1, keepdims=True
            )
        diagonal = lax.broadcasted_iota(jnp.int32, (capacity, LANES), 0) == lax.broadcasted_iota(
            jnp.int32, (capacity, LANES), 1
        )
        for n in range(experts):
            line = jnp.sum(
                jnp.where(diagonal, rho[n * capacity : (n + 1) * capacity], 0.0), axis=0, keepdims=True
            )
            target = rho_in if n == 0 else rho_out
            target[n] = jnp.broadcast_to(line, target.shape[1:])
        for copy in rho_copies():
            copy.start()

        @pl.loop(0, tiles + 1 + FINISH_LAG)
        def _(i):
            @pl.when(i + 1 < tiles)
            def _():
                load((0, 1), i + 1)

            @pl.when(i < tiles)
            def _():
                loaded((0, 1), i)
                slot = lax.rem(i, 2)
                total = dot_nt(gg[:, piece(0)], buf_g[slot, 0]) + dot_nt(ug[:, piece(0)], buf_u[slot, 0])
                for j in range(1, SLICES):
                    total += dot_nt(gg[:, piece(j)], buf_g[slot, j]) + dot_nt(ug[:, piece(j)], buf_u[slot, j])
                ship(1, i, total)

            @pl.when(i <= tiles)
            def _():
                relay_at(tiles + i - 1)

            finish_at(tiles + i - 1 - FINISH_LAG)

        def sent(block, sem):
            remote(block, block, sem, rho_r.at[0], device_of(pair)).wait_send()

        for which in range(3):
            weight, full, _ = weights[which]
            sent(weight, far_s.at[which])
            sent(full.at[1], cross_s.at[which])
            sent(weight, near_s.at[which])
        sent(own, raw_s)
        sent(info.at[0], info_s)
        for copy in rho_copies():
            copy.wait_send()

        @pl.when(inner)
        def _():
            sent(nbuf, nb_s)
            sent(stage.at[:, :, pl.ds(1, 1)], ret_s)
            sent(raw, cmb_s)

        @pl.when(outer)
        def _():
            sent(nbuf.at[:, :, pl.ds(0, 1)], nb_s)
            sent(stage.at[:, :, pl.ds(1, 3)], ret_s)

        for which, ref in enumerate((next_ref, prev_ref)):
            sent(obuf.at[which], out_s.at[which])
            remote(ref, ref, out_s.at[which], out_r.at[which], (after, me)).wait_recv()

    three = lambda value: jax.ShapeDtypeStruct((3,) + value.shape, value.dtype)
    in_vmem = pl.BlockSpec(memory_space=pltpu.VMEM)
    result = jax.ShapeDtypeStruct((token_count, width), BF16)
    dma = pltpu.SemaphoreType.DMA
    vmem = pltpu.VMEM
    wide = (rows, hidden)
    return pl.pallas_call(
        kernel,
        in_specs=[in_vmem] * 3 + [ANY] * 5,
        out_specs=[ANY] * 5,
        out_shape=[result] * 2 + [three(gate), three(up), three(down)],
        scratch_shapes=[
            vmem((2, token_count, width), BF16),
            vmem((2, tiles, experts, capacity, tile), BF16),
            vmem((2, tiles, 3, capacity, tile), BF16),
            vmem((2, tiles, 3, capacity, tile), BF16),
            vmem((2, tiles, 2, token_count, tile), BF16),
            vmem((2, tiles, token_count, tile), BF16),
            vmem((2, tiles, token_count, tile), BF16),
            vmem((3, 16, LANES), F32),
            vmem((LANES, LANES), F32),
            vmem((3, 2 * capacity, token_count), BF16),
            vmem((3, 2, token_count, capacity), BF16),
            vmem((3, 3, token_count, 1), F32),
            vmem((token_count, 1), F32),
            vmem((4, 8, LANES), F32),
            vmem((4, 8, LANES), F32),
        ]
        + [vmem(wide, F32)] * 3
        + [vmem(wide, BF16)] * 3
        + [vmem((2, SLICES, tile, ffd), BF16)] * 2
        + [vmem((2, SLICES, ffd, tile), BF16)]
        + [
            dma((2,)), dma, dma((2, tiles, 2)), dma, dma((2,)),
            dma, dma((2, tiles)), dma, dma((2, tiles)), dma, dma((2, tiles)),
            dma((3,)), dma((4,)), dma((2,)), dma((2,)),
            dma((3,)), dma((3, tiles)), dma((3,)), dma((3, tiles)), dma((3,)), dma((3,)),
            dma((3, 2, 2)),
        ],
        compiler_params=pltpu.CompilerParams(
            collective_id=1, has_side_effects=True, vmem_limit_bytes=VMEM
        ),
        name="relay_layer",
    )(ids, shares, gain, gate, up, down, tokens, grad_rows)[:2]


def slots_of(route_ids, home, experts, capacity):
    token_count, top_count = route_ids.shape
    relative = (route_ids.reshape(-1) - home + experts) % experts
    onehot = (relative[:, None] == jnp.arange(experts, dtype=jnp.int32)[None, :]).astype(jnp.int32)
    order = jnp.arange(onehot.shape[0], dtype=jnp.int32)
    earlier = (order[:, None] > order[None, :]).astype(BF16)
    before = dot_nn(earlier, onehot.astype(BF16)).astype(jnp.int32)
    target = relative * capacity + jnp.sum(before * onehot, axis=1)
    return target.reshape(token_count, top_count)


def pickers_of(pair_slot, experts, capacity):
    flat = pair_slot.T.reshape(-1)
    slots = jnp.arange(experts * capacity, dtype=jnp.int32).reshape(experts, 1, capacity)
    return (flat[None, :, None] == slots).astype(BF16)


def inverse_of(values):
    return lax.rsqrt(jnp.mean(values * values, axis=-1, keepdims=True) + EPSILON)


def body(tokens, grad_out, norm_gain, expert_ids, gate_weights, w_gate, w_up, w_down):
    tokens = tokens[0]
    grad_rows = grad_out[0]
    gain = norm_gain[0][None, :]
    route_ids = expert_ids[0]
    route_weights = gate_weights[0]
    token_count, width = tokens.shape
    top_count = route_ids.shape[1]
    devices = lax.axis_size("expert")
    pipes = lax.axis_size("pipe")
    experts = devices // SLICES
    step_size = 4 * experts * SLICES
    capacity = min(
        token_count, SLICES * ((token_count * top_count * 5 + step_size - 1) // step_size)
    )
    home = lax.axis_index("expert") // SLICES
    same = lambda d: d

    gate, up, down = w_gate[0], w_up[0], w_down[0]

    if experts == 4 and token_count == LANES:
        next_rows, prev_rows = relay_layer(
            route_ids.T, route_weights.T, gain, gate, up, down, tokens, grad_rows, capacity, top_count
        )
        return (next_rows[None], prev_rows[None])

    values = tokens.astype(F32)
    inverse = inverse_of(values)
    pair_slot = slots_of(route_ids, home, experts, capacity)
    picker = jnp.any(
        pair_slot[None, :, :]
        == jnp.arange(experts * capacity, dtype=jnp.int32)[:, None, None],
        axis=2,
    ).astype(BF16)

    routing = jnp.concatenate([pair_slot.astype(F32), route_weights, inverse], axis=1)
    routing_next = move(routing, 1, same)
    routing_prev = routing_next if pipes == 2 else move(routing, -1, same)
    gain_prev = move(gain, -1, same)

    def routing_of(table):
        slots = table[:, :top_count].astype(jnp.int32)
        return pickers_of(slots, experts, capacity), table[:, top_count : 2 * top_count]

    pick_next, weights_next = routing_of(routing_next)
    pick_prev, weights_prev = routing_of(routing_prev)
    next_rows, prev_rows = layer(
        picker, inverse, gain, gate, up, down, tokens, grad_rows,
        gain_prev, routing_prev[:, 2 * top_count :],
        pick_next, weights_next, pick_prev, weights_prev,
    )
    return (next_rows[None], prev_rows[None])


def solution(mesh):
    return jax.shard_map(
        body,
        mesh=mesh,
        in_specs=(
            P("pipe", "expert", None),
            P("pipe", "expert", None),
            P("pipe", None),
            P("pipe", "expert", None),
            P("pipe", "expert", None),
            P("pipe", None, "expert"),
            P("pipe", None, "expert"),
            P("pipe", "expert", None),
        ),
        out_specs=(P("pipe", "expert", None), P("pipe", "expert", None)),
        check_vma=False,
    )
```

```python
import jax
import jax.numpy as jnp
from jax import lax
from jax.experimental import pallas as pl
from jax.experimental.pallas import tpu as pltpu
from jax.sharding import PartitionSpec as P

SLICES = 4
EPSILON = 1e-06
BF16 = jnp.bfloat16
F32 = jnp.float32


def move(value, pipe_steps, expert_map):
    pipes, devices = lax.axis_size("pipe"), lax.axis_size("expert")
    pairs = [
        (p * devices + d, ((p + pipe_steps) % pipes) * devices + expert_map(d))
        for p in range(pipes)
        for d in range(devices)
    ]
    return lax.ppermute(value, ("pipe", "expert"), pairs)


def dot_nt(left_arr, right_arr):
    return lax.dot_general(
        left_arr, right_arr, (((1,), (1,)), ((), ())), preferred_element_type=F32
    )


def dot_nn(left_arr, right_arr):
    return jnp.dot(left_arr, right_arr, preferred_element_type=F32)


def tile_of(width):
    for tile in (1024, 512, 256, 128):
        if width % tile == 0:
            return tile
    return width


MESH = pl.DeviceIdType.MESH
ANY = pl.BlockSpec(memory_space=pl.ANY)


def sections():
    pipe, pipes = lax.axis_index("pipe"), lax.axis_size("pipe")
    return pipe, lax.rem(pipe + 1, pipes), lax.rem(pipe + pipes - 1, pipes)


def greet(partners):
    barrier = pltpu.get_barrier_semaphore()
    for partner in partners:
        pl.semaphore_signal(barrier, inc=1, device_id=partner, device_id_type=MESH)
    pl.semaphore_wait(barrier, len(partners))


VMEM = 62 * 1024 * 1024


def layer(picker, inverse, gain, gate, up, down, tokens, grad_rows,
          gain_prev, inverse_prev, pick_next, wt_next, pick_prev, wt_prev):
    rows = picker.shape[0]
    experts, _, capacity = pick_next.shape
    width = tokens.shape[1]
    ffd = down.shape[0]
    token_count, top = wt_next.shape
    devices, pipes = lax.axis_size("expert"), lax.axis_size("pipe")
    tile = tile_of(width)
    tiles = width // tile

    def kernel(pick, inv_own, gain_own, wg, wu, wd, tok, grd, gain, inv, pn, wn, pp, wp,
               next_ref, prev_ref, ag, au, ad,
               ri, rg, si, sg, tn, tp, gp, recv_o, recv_g, scaled, acc_g, acc_u, acc_h, hid, gg, ug,
               buf_g, buf_u, buf_d,
               far_s, far_r, cross_s, cross_r, near_s, near_r, rows_s, rows_r, tok_s, tok_r,
               load_sem, send, recv):
        pipe, after, ahead = sections()
        me = lax.axis_index("expert")
        place = lax.rem(me, SLICES)
        far = me - place + lax.rem(place + 2, SLICES)
        near = me + 1 - 2 * lax.rem(me, 2)
        others = [lax.rem(me + SLICES * s, devices) for s in range(1, experts)]
        homes = [lax.rem(me + devices - SLICES * s, devices) for s in range(experts)]
        greet(
            [(pipe, d) for d in others]
            + [(pipe, far), (pipe, near)]
            + [(p, d) for p in (after, ahead) for d in homes]
        )
        weights = ((wg, ag, buf_g), (wu, au, buf_u), (wd, ad, buf_d))
        stages = (ri, rg)

        def remote(source, target, send_sem, recv_sem, device):
            return pltpu.make_async_remote_copy(
                src_ref=source, dst_ref=target, send_sem=send_sem, recv_sem=recv_sem,
                device_id=device, device_id_type=MESH,
            )

        def cols_of(i):
            return pl.ds(pl.multiple_of(i * tile, tile), tile)

        def part(ref, which, i):
            return ref.at[cols_of(i), :] if which < 2 else ref.at[:, cols_of(i)]

        def far_copy(which, i):
            own, full, _ = weights[which]
            return remote(
                part(own, which, i), part(full.at[1], which, i),
                far_s.at[which, i], far_r.at[which, i], (pipe, far),
            )

        def cross_copy(which, i):
            full = weights[which][1]
            return remote(
                part(full.at[1], which, i), part(full.at[2], which, i),
                cross_s.at[which, i], cross_r.at[which, i], (pipe, near),
            )

        def near_copy(which):
            own, full, _ = weights[which]
            return remote(own, full.at[0], near_s.at[which], near_r.at[which], (pipe, near))

        def row_copy(which, i, s):
            return remote(
                (si, sg)[which].at[s - 1, :, cols_of(i)], stages[which].at[s, :, cols_of(i)],
                rows_s.at[which, i, s - 1], rows_r.at[which, i, s - 1], (pipe, others[s - 1]),
            )

        def token_copies():
            moves = [(tok, tn, after), (grd, gp, ahead), (tok, tp, ahead)]
            return [
                remote(source, target, tok_s.at[n], tok_r.at[n], (device, me))
                for n, (source, target, device) in enumerate(moves)
            ]

        def loads(which, i):
            own, full, buf = weights[which]
            slot = lax.rem(i, 2)
            return [
                pltpu.make_async_copy(
                    part(own if j == 0 else full.at[j - 1], which, i),
                    buf.at[slot, j],
                    load_sem.at[which, slot, j],
                )
                for j in range(SLICES)
            ]

        def load(kinds, i):
            for which in kinds:
                for copy in loads(which, i):
                    copy.start()

        def loaded(kinds, i):
            for which in kinds:
                for copy in loads(which, i):
                    copy.wait()

        def result_copy(which, i, s):
            return remote(
                stages[which].at[s, :, cols_of(i)], (recv_o, recv_g)[which].at[s, :, cols_of(i)],
                send.at[which, i, s], recv.at[which, i, s], ((after, ahead)[which], homes[s]),
            )

        def ship(which, i, total):
            for s in range(experts):
                stages[which][s, :, cols_of(i)] = total[s * capacity : (s + 1) * capacity].astype(BF16)
            for s in range(experts):
                result_copy(which, i, s).start()

        def send_rows(which, i):
            cols = cols_of(i)
            value = tok[:, cols].astype(F32) * inv_own[...] * gain_own[:, cols] if which == 0 else grd[:, cols]
            slots = dot_nn(pick[...], value.astype(BF16))
            stages[which][0, :, cols] = slots[:capacity].astype(BF16)
            for s in range(1, experts):
                (si, sg)[which][s - 1, :, cols] = slots[s * capacity : (s + 1) * capacity].astype(BF16)
            for s in range(experts - 1, 0, -1):
                row_copy(which, i, s).start()

        def send_far(kinds, i):
            for which in kinds:
                far_copy(which, i).start()

        def tile_rows(which, i):
            return stages[which][:, :, cols_of(i)].reshape(rows, tile)

        def piece(j):
            return slice(j * ffd, (j + 1) * ffd)

        first_far, first_down = min(2, tiles), min(4, tiles)
        for i in range(first_far):
            send_far((0, 1), i)

        @pl.loop(0, tiles)
        def _(i):
            send_rows(0, i)

        for which in range(3):
            near_copy(which).start()
        for copy in token_copies():
            copy.start()
        acc_g[...] = jnp.zeros_like(acc_g)
        acc_u[...] = jnp.zeros_like(acc_u)
        acc_h[...] = jnp.zeros_like(acc_h)
        near_copy(0).wait()
        near_copy(1).wait()

        def pipeline(kinds, arrive, compute):
            @pl.loop(0, tiles + 2)
            def _(i):
                @pl.when(i < tiles)
                def _():
                    arrive(i)
                    for which in kinds:
                        far_copy(which, i).wait()
                        cross_copy(which, i).start()

                @pl.when((i >= 1) & (i <= tiles))
                def _():
                    for which in kinds:
                        cross_copy(which, i - 1).wait()
                    load(kinds, i - 1)

                @pl.when(i >= 2)
                def _():
                    loaded(kinds, i - 2)
                    compute(i - 2)

        def arrive_first(i):
            send_rows(1, i)

            @pl.when(i + first_far < tiles)
            def _():
                send_far((0, 1), i + first_far)

            @pl.when(i == tiles - 1)
            def _():
                for n in range(first_down):
                    send_far((2,), n)

        def compute_first(i):
            for s in range(1, experts):
                row_copy(0, i, s).wait()
            slot = lax.rem(i, 2)
            block = tile_rows(0, i)
            for j in range(SLICES):
                acc_g[:, piece(j)] += dot_nn(block, buf_g[slot, j])
                acc_u[:, piece(j)] += dot_nn(block, buf_u[slot, j])

        pipeline((0, 1), arrive_first, compute_first)

        for j in range(SLICES):
            gate_pre = acc_g[:, piece(j)]
            hid[:, piece(j)] = (gate_pre * jax.nn.sigmoid(gate_pre) * acc_u[:, piece(j)]).astype(BF16)
        near_copy(2).wait()

        def arrive_down(i):
            @pl.when(i + first_down < tiles)
            def _():
                send_far((2,), i + first_down)

        def compute_down(i):
            slot = lax.rem(i, 2)
            total = dot_nn(hid[:, piece(0)], buf_d[slot, 0])
            for j in range(1, SLICES):
                total += dot_nn(hid[:, piece(j)], buf_d[slot, j])
            ship(0, i, total)
            for s in range(1, experts):
                row_copy(1, i, s).wait()
            block = tile_rows(1, i)
            for j in range(SLICES):
                acc_h[:, piece(j)] += dot_nt(block, buf_d[slot, j])

        pipeline((2,), arrive_down, compute_down)

        load((0, 1), 0)
        for j in range(SLICES):
            gate_pre, up_pre, grad_hidden = acc_g[:, piece(j)], acc_u[:, piece(j)], acc_h[:, piece(j)]
            sig = jax.nn.sigmoid(gate_pre)
            gg[:, piece(j)] = (grad_hidden * up_pre * sig * (1.0 + gate_pre * (1.0 - sig))).astype(BF16)
            ug[:, piece(j)] = (grad_hidden * (gate_pre * sig)).astype(BF16)

        @pl.loop(0, tiles)
        def _(i):
            @pl.when(i + 1 < tiles)
            def _():
                load((0, 1), i + 1)

            loaded((0, 1), i)
            slot = lax.rem(i, 2)
            total = dot_nt(gg[:, piece(0)], buf_g[slot, 0]) + dot_nt(ug[:, piece(0)], buf_u[slot, 0])
            for j in range(1, SLICES):
                total += dot_nt(gg[:, piece(j)], buf_g[slot, j]) + dot_nt(ug[:, piece(j)], buf_u[slot, j])
            ship(1, i, total)

        def picked(target, pick, scale, cols):
            total = dot_nn(pick[0], target[0, :, cols])
            for s in range(1, experts):
                total += dot_nn(pick[s], target[s, :, cols])
            value = total[:token_count] * scale[:, 0:1]
            for n in range(1, top):
                value += total[n * token_count : (n + 1) * token_count] * scale[:, n : n + 1]
            return value

        for copy in token_copies():
            copy.wait()

        @pl.loop(0, tiles)
        def _(i):
            cols = cols_of(i)
            for s in range(experts):
                result_copy(0, i, s).wait()
            next_ref[:, cols] = (tn[:, cols].astype(F32) + picked(recv_o, pn, wn, cols)).astype(BF16)

        def finish(i, mean):
            cols = cols_of(i)
            for s in range(experts):
                result_copy(1, i, s).wait()
            value = picked(recv_g, pp, wp, cols) * gain[:, cols]
            scaled[:, cols] = value
            return mean + jnp.sum(value * tp[:, cols].astype(F32), axis=1, keepdims=True)

        mean = lax.fori_loop(0, tiles, finish, jnp.zeros((token_count, 1), F32)) / width
        inverse = inv[...]
        factor = inverse * inverse * inverse * mean

        @pl.loop(0, tiles)
        def _(i):
            cols = cols_of(i)
            prev_ref[:, cols] = (
                gp[:, cols].astype(F32) + inverse * scaled[:, cols] - tp[:, cols].astype(F32) * factor
            ).astype(BF16)

    three = lambda value: jax.ShapeDtypeStruct((3,) + value.shape, value.dtype)
    in_vmem = pl.BlockSpec(memory_space=pltpu.VMEM)
    result = jax.ShapeDtypeStruct((token_count, width), BF16)
    row_block = pltpu.VMEM((experts, capacity, width), BF16)
    token_block = pltpu.VMEM((token_count, width), BF16)
    wide = (rows, SLICES * ffd)
    dma = pltpu.SemaphoreType.DMA
    return pl.pallas_call(
        kernel,
        in_specs=[in_vmem] * 3 + [ANY] * 3 + [in_vmem] * 8,
        out_specs=[in_vmem] * 2 + [ANY] * 3,
        out_shape=[result] * 2 + [three(gate), three(up), three(down)],
        scratch_shapes=[row_block] * 2
        + [pltpu.VMEM((experts - 1, capacity, width), BF16)] * 2
        + [token_block] * 3
        + [row_block] * 2
        + [pltpu.VMEM((token_count, width), F32)]
        + [pltpu.VMEM(wide, F32)] * 3
        + [pltpu.VMEM(wide, BF16)] * 3
        + [pltpu.VMEM((2, SLICES, tile, ffd), BF16)] * 2
        + [pltpu.VMEM((2, SLICES, ffd, tile), BF16)]
        + [dma((3, tiles))] * 4
        + [dma((3,))] * 2
        + [dma((2, tiles, experts - 1))] * 2
        + [dma((3,))] * 2
        + [dma((3, 2, SLICES))]
        + [dma((2, tiles, experts))] * 2,
        compiler_params=pltpu.CompilerParams(
            collective_id=0, has_side_effects=True, vmem_limit_bytes=VMEM
        ),
        name="layer",
    )(picker, inverse, gain, gate, up, down, tokens, grad_rows,
      gain_prev, inverse_prev, pick_next, wt_next, pick_prev, wt_prev)[:2]


LANES = 128
TILE = 256
AHEAD = 6
FAR_AHEAD = 4
DOWN_AHEAD = 8
FINISH_LAG = 2


def relay_layer(ids, shares, gain, gate, up, down, tokens, grad_rows, capacity, top):
    experts = 4
    token_count, width = tokens.shape
    ffd = down.shape[0]
    hidden = SLICES * ffd
    rows = experts * capacity
    devices = lax.axis_size("expert")
    tile = min(TILE, tile_of(width))
    tiles = width // tile
    units = 2 * tiles

    def kernel(ids_ref, shares_ref, gain_ref, wg, wu, wd, tok, grd,
               next_ref, prev_ref, ag, au, ad,
               own, stage, nbuf, rbuf, raw, cbuf, obuf, info, square, pick, back, scale, coef,
               rho_out, rho_in, acc_g, acc_u, acc_h, hid, gg, ug, buf_g, buf_u, buf_d,
               own_l, raw_s, raw_r, info_s, info_r, nb_s, nb_r, ret_s, ret_r, cmb_s, cmb_r,
               rho_s, rho_r, out_s, out_r, far_s, far_r, cross_s, cross_r, near_s, near_r, load_sem):
        pipe, after, ahead = sections()
        me = lax.axis_index("expert")
        place = lax.rem(me, SLICES)
        mine = lax.div(me, SLICES)
        half = lax.div(mine, 2)
        outer_index = 1 - lax.rem(lax.div(mine + 1, 2), 2)
        inner = outer_index == 0
        outer = outer_index == 1
        far = me - place + lax.rem(place + 2, SLICES)
        near = me + 1 - 2 * lax.rem(me, 2)

        def device_of(expert):
            return (pipe, expert * SLICES + place)

        pair = mine + 1 - 2 * lax.rem(mine, 2)
        opposite = [2 - half, 3 - 3 * half]
        greet(
            [(pipe, lax.rem(me + SLICES * s, devices)) for s in range(1, experts)]
            + [(pipe, far), (pipe, near), (after, me), (ahead, me)]
        )
        weights = ((wg, ag, buf_g), (wu, au, buf_u), (wd, ad, buf_d))

        def remote(source, target, send_sem, recv_sem, device):
            return pltpu.make_async_remote_copy(
                src_ref=source, dst_ref=target, send_sem=send_sem, recv_sem=recv_sem,
                device_id=device, device_id_type=MESH,
            )

        def cols_of(i):
            return pl.ds(pl.multiple_of(i * tile, tile), tile)

        def part(ref, which, i):
            return ref.at[cols_of(i), :] if which < 2 else ref.at[:, cols_of(i)]

        def far_copy(which, i):
            weight, full, _ = weights[which]
            return remote(
                part(weight, which, i), part(full.at[1], which, i),
                far_s.at[which], far_r.at[which, i], (pipe, far),
            )

        def cross_copy(which, i):
            full = weights[which][1]
            return remote(
                part(full.at[1], which, i), part(full.at[2], which, i),
                cross_s.at[which], cross_r.at[which, i], (pipe, near),
            )

        def near_copy(which):
            weight, full, _ = weights[which]
            return remote(weight, full.at[0], near_s.at[which], near_r.at[which], (pipe, near))

        def loads(which, i):
            weight, full, buf = weights[which]
            slot = lax.rem(i, 2)
            cols = cols_of(i)
            if which < 2:
                return [
                    pltpu.make_async_copy(
                        part(weight if j == 0 else full.at[j - 1], which, i),
                        buf.at[slot, :, pl.ds(j * ffd, ffd)],
                        load_sem.at[which, slot, j],
                    )
                    for j in range(SLICES)
                ]
            gathered = full.at[:, :, cols]
            return [
                pltpu.make_async_copy(part(weight, which, i), buf.at[slot, 0], load_sem.at[which, slot, 0]),
                pltpu.make_async_copy(gathered, buf.at[slot, pl.ds(1, SLICES - 1)], load_sem.at[which, slot, 1]),
            ]

        def load(kinds, i):
            for which in kinds:
                for copy in loads(which, i):
                    copy.start()

        def loaded(kinds, i):
            for which in kinds:
                for copy in loads(which, i):
                    copy.wait()

        def split(u):
            return lax.div(u, tiles), lax.rem(u, tiles)

        def raw_copy(source, which, i):
            return remote(
                source, raw.at[which, i, outer_index], raw_s, raw_r.at[which, i, outer_index],
                device_of(opposite[0]),
            )

        def raw_start(u):
            which, i = split(u)
            raw_copy(own.at[which, :, cols_of(i)], which, i).start()

        def raw_wait(which, i, n):
            block = raw.at[which, i, n]
            remote(block, block, raw_s, raw_r.at[which, i, n], device_of(opposite[0])).wait_recv()

        def info_copy():
            return remote(
                info.at[0], info.at[1 + outer_index], info_s, info_r.at[outer_index], device_of(opposite[0])
            )

        def info_wait(n):
            block = info.at[1 + n]
            remote(block, block, info_s, info_r.at[n], device_of(opposite[0])).wait_recv()

        def nb_copy(which, i, blocks):
            return remote(
                nbuf.at[which, i, pl.ds(0, blocks)], stage.at[which, i, pl.ds(1, blocks)],
                nb_s, nb_r.at[which, i], device_of(pair),
            )

        def ret_copy(which, i, blocks):
            return remote(
                stage.at[which, i, pl.ds(1, blocks)], rbuf.at[which, i, pl.ds(0, blocks)],
                ret_s, ret_r.at[which, i], device_of(pair),
            )

        def cmb_copy(which, i, n):
            return remote(
                raw.at[which, i, n], cbuf.at[which, i], cmb_s, cmb_r.at[which, i], device_of(opposite[n])
            )

        def out_copy(which, i):
            return remote(
                obuf.at[which, i], (next_ref, prev_ref)[which].at[:, cols_of(i)],
                out_s.at[which], out_r.at[which], ((after, ahead)[which], me),
            )

        def rho_copies():
            places = (1, 2 + outer_index, 2 + outer_index)
            targets = (pair, opposite[0], opposite[1])
            return [
                remote(rho_out.at[n + 1], rho_in.at[places[n]], rho_s.at[n], rho_r.at[places[n]], device_of(targets[n]))
                for n in range(3)
            ]

        def rho_wait(n):
            block = rho_in.at[n]
            remote(block, block, rho_s.at[0], rho_r.at[n], device_of(pair)).wait_recv()

        own_loads = [
            pltpu.make_async_copy(source, own.at[n], own_l.at[n]) for n, source in enumerate((tok, grd))
        ]

        def piece(j):
            return slice(j * ffd, (j + 1) * ffd)

        for copy in own_loads:
            copy.start()
        first_raw = min(2, tiles)
        for i in range(min(FAR_AHEAD, tiles)):
            for which in (0, 1):
                far_copy(which, i).start()
            if i < first_raw:
                raw_copy(tok.at[:, cols_of(i)], 0, i).start()
        near_copy(0).start()
        near_copy(1).start()

        lane = lax.broadcasted_iota(jnp.int32, (token_count, LANES), 1)
        lane_value = lane.astype(F32)

        def full_of(n):
            square[...] = jnp.zeros_like(square)
            square[: info.shape[1]] = info[n]
            return square[...].T

        def column(full, index):
            return jnp.sum(jnp.where(lane == index, full, 0.0), axis=1, keepdims=True)

        def set_tables(n):
            full = full_of(n)
            slot = lax.broadcasted_iota(jnp.int32, (capacity, token_count), 0).astype(F32)
            slot_lane = lax.broadcasted_iota(jnp.int32, (token_count, capacity), 1).astype(F32)
            for k, expert in enumerate((mine, pair)):
                pick[n, k * capacity : (k + 1) * capacity] = (slot == info[n, pl.ds(expert, 1), :]).astype(BF16)
                back[n, k] = (slot_lane == column(full, expert)).astype(BF16)
                scale[n, k] = column(full, experts + expert)
            scale[n, 2] = column(full, 2 * experts)

        own_loads[0].wait()

        def add_squares(i, total):
            value = own[0, :, cols_of(i)].astype(F32)
            return total + jnp.sum(value * value, axis=1, keepdims=True)

        squares = lax.fori_loop(0, tiles, add_squares, jnp.zeros((token_count, 1), F32))
        inverse_own = lax.rsqrt(squares / width + EPSILON)
        expert_row = lax.broadcasted_iota(jnp.int32, (8, LANES), 0)
        hit = jnp.zeros((8, LANES), F32)
        weight_of = jnp.zeros((8, LANES), F32)
        for k in range(top):
            named = expert_row == ids_ref[k : k + 1]
            hit += jnp.where(named, 1.0, 0.0)
            weight_of += jnp.where(named, shares_ref[k : k + 1], 0.0)
        earlier = (lax.broadcasted_iota(jnp.int32, (token_count, LANES), 0) < lane).astype(BF16)
        before = dot_nn(hit.astype(BF16), earlier)
        square[...] = jnp.zeros_like(square)
        square[:experts] = jnp.where(hit > 0.5, before, -1.0)[:experts]
        square[experts : 2 * experts] = weight_of[:experts]
        full_own = jnp.where(lane == 2 * experts, inverse_own, square[...].T)
        info[0] = full_own.T[: info.shape[1]]
        info_copy().start()
        own_loads[1].wait()
        for u in range(first_raw, min(AHEAD, units)):
            raw_start(u)
        set_tables(0)
        acc_g[...] = jnp.zeros_like(acc_g)
        acc_u[...] = jnp.zeros_like(acc_u)
        acc_h[...] = jnp.zeros_like(acc_h)

        @pl.when(inner)
        def _():
            for n in range(2):
                info_wait(n)
                set_tables(n + 1)

        def dispatch(u):
            which, i = split(u)
            gain_row = jnp.where(which == 0, gain_ref[:, cols_of(i)], 1.0)

            def slots(n, value):
                factor = jnp.where(which == 0, scale[n, 2], 1.0)
                return dot_nn(pick[n], (value.astype(F32) * factor * gain_row).astype(BF16)).astype(BF16)

            taken = slots(0, own[which, :, cols_of(i)])
            stage[which, i, 0] = taken[:capacity]
            nbuf[which, i, 0] = taken[capacity:]

            @pl.when(inner)
            def _():
                for n in range(2):
                    raw_wait(which, i, n)
                    passed = slots(n + 1, raw[which, i, n])
                    stage[which, i, n + 2] = passed[:capacity]
                    nbuf[which, i, n + 1] = passed[capacity:]
                nb_copy(which, i, 3).start()

            @pl.when(outer)
            def _():
                nb_copy(which, i, 1).start()

        def nb_wait(which, i):
            @pl.when(inner)
            def _():
                nb_copy(which, i, 1).wait_recv()

            @pl.when(outer)
            def _():
                nb_copy(which, i, 3).wait_recv()

        def tile_rows(which, i):
            return stage[which, i].reshape(rows, tile)

        @pl.loop(0, tiles + 1)
        def _(i):
            @pl.when((i >= 1) & (i < tiles))
            def _():
                for n in range(2):
                    u = 2 * (i - 1) + n

                    @pl.when(u + AHEAD < units)
                    def _():
                        raw_start(u + AHEAD)

                    dispatch(u)

            @pl.when(i >= 1)
            def _():
                t = i - 1
                nb_wait(0, t)
                loaded((0, 1), t)
                slot = lax.rem(t, 2)
                block = tile_rows(0, t)
                acc_g[...] += dot_nn(block, buf_g[slot])
                acc_u[...] += dot_nn(block, buf_u[slot])

            @pl.when(i < tiles)
            def _():
                for which in (0, 1):
                    far_copy(which, i).wait_recv()
                    cross_copy(which, i).start()

                @pl.when(i + FAR_AHEAD < tiles)
                def _():
                    for which in (0, 1):
                        far_copy(which, i + FAR_AHEAD).start()

                @pl.when(i + FAR_AHEAD >= tiles)
                def _():
                    for n in range(2):
                        d = 2 * (i - max(tiles - FAR_AHEAD, 0)) + n

                        @pl.when(d < min(DOWN_AHEAD, tiles))
                        def _():
                            far_copy(2, d).start()

                @pl.when(i == min(4, tiles - 1))
                def _():
                    near_copy(2).start()

                @pl.when(i == 0)
                def _():
                    near_copy(0).wait_recv()
                    near_copy(1).wait_recv()

                for which in (0, 1):
                    cross_copy(which, i).wait_recv()
                load((0, 1), i)

        near_copy(2).wait_recv()
        far_copy(2, 0).wait_recv()
        cross_copy(2, 0).start()
        for j in range(SLICES):
            gate_pre = acc_g[:, piece(j)]
            hid[:, piece(j)] = (gate_pre * jax.nn.sigmoid(gate_pre) * acc_u[:, piece(j)]).astype(BF16)

        def ship(which, i, total):
            stage[which, i] = total.astype(BF16).reshape(experts, capacity, tile)

            @pl.when(inner)
            def _():
                ret_copy(which, i, 1).start()

            @pl.when(outer)
            def _():
                ret_copy(which, i, 3).start()

        def relay(u):
            which, i = split(u)
            ret_copy(which, i, 3).wait_recv()
            for n in range(2):
                value = scale[n + 1, 0] * dot_nn(back[n + 1, 0], stage[which, i, n + 2])
                value += scale[n + 1, 1] * dot_nn(back[n + 1, 1], rbuf[which, i, n + 1])
                raw[which, i, n] = value.astype(BF16)
                cmb_copy(which, i, n).start()

        def finish(u):
            which, i = split(u)
            cols = cols_of(i)

            @pl.when(outer)
            def _():
                ret_copy(which, i, 1).wait_recv()

            cmb_copy(which, i, 0).wait_recv()
            value = cbuf[which, i].astype(F32)
            value += scale[0, 0] * dot_nn(back[0, 0], stage[which, i, 0])
            value += scale[0, 1] * dot_nn(back[0, 1], rbuf[which, i, 0])

            @pl.when(which == 0)
            def _():
                obuf[0, i] = (own[0, :, cols].astype(F32) + value).astype(BF16)
                out_copy(0, i).start()

            @pl.when(which == 1)
            def _():
                @pl.when(i == 0)
                def _():
                    full = full_of(0)
                    total = jnp.zeros((token_count, 1), F32)
                    for n, expert in enumerate((mine, pair, opposite[0], opposite[1])):
                        if n > 0:
                            rho_wait(n)
                        found = lane_value == column(full, expert)
                        taken = jnp.sum(jnp.where(found, rho_in[n, 0:1], 0.0), axis=1, keepdims=True)
                        total += column(full, experts + expert) * taken
                    coef[...] = scale[0, 2] * scale[0, 2] * total / width

                grown = scale[0, 2] * (value * gain_ref[:, cols])
                obuf[1, i] = (
                    own[1, :, cols].astype(F32) + grown - own[0, :, cols].astype(F32) * coef[...]
                ).astype(BF16)
                out_copy(1, i).start()

        def relay_at(u):
            @pl.when((u >= 0) & inner)
            def _():
                relay(u)

        def finish_at(u):
            @pl.when((u >= 0) & (u < units))
            def _():
                finish(u)

        cross_copy(2, 0).wait_recv()
        load((2,), 0)

        @pl.loop(0, tiles)
        def _(i):
            slot = lax.rem(i, 2)
            loaded((2,), i)
            ship(0, i, dot_nn(hid[...], buf_d[slot].reshape(hidden, tile)))

            @pl.when(i + 1 < tiles)
            def _():
                far_copy(2, i + 1).wait_recv()
                cross_copy(2, i + 1).start()

                @pl.when(i + DOWN_AHEAD < tiles)
                def _():
                    far_copy(2, i + DOWN_AHEAD).start()

            nb_wait(1, i)
            acc_h[...] += dot_nt(tile_rows(1, i), buf_d[slot].reshape(hidden, tile))

            @pl.when(i + 1 < tiles)
            def _():
                cross_copy(2, i + 1).wait_recv()
                load((2,), i + 1)

            @pl.when(i < 2)
            def _():
                dispatch(units - 2 + i)

            relay_at(i - 1)
            finish_at(i - 1 - FINISH_LAG)

        load((0, 1), 0)
        rho = jnp.zeros((rows, 1), F32)
        for j in range(SLICES):
            gate_pre, up_pre, grad_hidden = acc_g[:, piece(j)], acc_u[:, piece(j)], acc_h[:, piece(j)]
            sig = jax.nn.sigmoid(gate_pre)
            grad_gate = (grad_hidden * up_pre * sig * (1.0 + gate_pre * (1.0 - sig))).astype(BF16)
            grad_up = (grad_hidden * (gate_pre * sig)).astype(BF16)
            gg[:, piece(j)] = grad_gate
            ug[:, piece(j)] = grad_up
            rho += jnp.sum(
                grad_gate.astype(F32) * gate_pre + grad_up.astype(F32) * up_pre, axis=1, keepdims=True
            )
        diagonal = lax.broadcasted_iota(jnp.int32, (capacity, LANES), 0) == lax.broadcasted_iota(
            jnp.int32, (capacity, LANES), 1
        )
        for n in range(experts):
            line = jnp.sum(
                jnp.where(diagonal, rho[n * capacity : (n + 1) * capacity], 0.0), axis=0, keepdims=True
            )
            target = rho_in if n == 0 else rho_out
            target[n] = jnp.broadcast_to(line, target.shape[1:])
        for copy in rho_copies():
            copy.start()

        @pl.loop(0, tiles + 1 + FINISH_LAG)
        def _(i):
            @pl.when(i + 1 < tiles)
            def _():
                load((0, 1), i + 1)

            @pl.when(i < tiles)
            def _():
                loaded((0, 1), i)
                slot = lax.rem(i, 2)
                ship(1, i, dot_nt(gg[...], buf_g[slot]) + dot_nt(ug[...], buf_u[slot]))

            @pl.when(i <= tiles)
            def _():
                relay_at(tiles + i - 1)

            finish_at(tiles + i - 1 - FINISH_LAG)

        def sent(block, sem):
            remote(block, block, sem, rho_r.at[0], device_of(pair)).wait_send()

        for which in range(3):
            weight, full, _ = weights[which]
            sent(weight, far_s.at[which])
            sent(full.at[1], cross_s.at[which])
            sent(weight, near_s.at[which])
        sent(own, raw_s)
        sent(info.at[0], info_s)
        for copy in rho_copies():
            copy.wait_send()

        @pl.when(inner)
        def _():
            sent(nbuf, nb_s)
            sent(stage.at[:, :, pl.ds(1, 1)], ret_s)
            sent(raw, cmb_s)

        @pl.when(outer)
        def _():
            sent(nbuf.at[:, :, pl.ds(0, 1)], nb_s)
            sent(stage.at[:, :, pl.ds(1, 3)], ret_s)

        for which, ref in enumerate((next_ref, prev_ref)):
            sent(obuf.at[which], out_s.at[which])
            remote(ref, ref, out_s.at[which], out_r.at[which], (after, me)).wait_recv()

    three = lambda value: jax.ShapeDtypeStruct((3,) + value.shape, value.dtype)
    in_vmem = pl.BlockSpec(memory_space=pltpu.VMEM)
    result = jax.ShapeDtypeStruct((token_count, width), BF16)
    dma = pltpu.SemaphoreType.DMA
    vmem = pltpu.VMEM
    wide = (rows, hidden)
    return pl.pallas_call(
        kernel,
        in_specs=[in_vmem] * 3 + [ANY] * 5,
        out_specs=[ANY] * 5,
        out_shape=[result] * 2 + [three(gate), three(up), three(down)],
        scratch_shapes=[
            vmem((2, token_count, width), BF16),
            vmem((2, tiles, experts, capacity, tile), BF16),
            vmem((2, tiles, 3, capacity, tile), BF16),
            vmem((2, tiles, 3, capacity, tile), BF16),
            vmem((2, tiles, 2, token_count, tile), BF16),
            vmem((2, tiles, token_count, tile), BF16),
            vmem((2, tiles, token_count, tile), BF16),
            vmem((3, 16, LANES), F32),
            vmem((LANES, LANES), F32),
            vmem((3, 2 * capacity, token_count), BF16),
            vmem((3, 2, token_count, capacity), BF16),
            vmem((3, 3, token_count, 1), F32),
            vmem((token_count, 1), F32),
            vmem((4, 8, LANES), F32),
            vmem((4, 8, LANES), F32),
        ]
        + [vmem(wide, F32)] * 3
        + [vmem(wide, BF16)] * 3
        + [vmem((2, tile, hidden), BF16)] * 2
        + [vmem((2, SLICES, ffd, tile), BF16)]
        + [
            dma((2,)), dma, dma((2, tiles, 2)), dma, dma((2,)),
            dma, dma((2, tiles)), dma, dma((2, tiles)), dma, dma((2, tiles)),
            dma((3,)), dma((4,)), dma((2,)), dma((2,)),
            dma((3,)), dma((3, tiles)), dma((3,)), dma((3, tiles)), dma((3,)), dma((3,)),
            dma((3, 2, SLICES)),
        ],
        compiler_params=pltpu.CompilerParams(
            collective_id=1, has_side_effects=True, vmem_limit_bytes=VMEM
        ),
        name="relay_layer",
    )(ids, shares, gain, gate, up, down, tokens, grad_rows)[:2]


def slots_of(route_ids, home, experts, capacity):
    token_count, top_count = route_ids.shape
    relative = (route_ids.reshape(-1) - home + experts) % experts
    onehot = (relative[:, None] == jnp.arange(experts, dtype=jnp.int32)[None, :]).astype(jnp.int32)
    order = jnp.arange(onehot.shape[0], dtype=jnp.int32)
    earlier = (order[:, None] > order[None, :]).astype(BF16)
    before = dot_nn(earlier, onehot.astype(BF16)).astype(jnp.int32)
    target = relative * capacity + jnp.sum(before * onehot, axis=1)
    return target.reshape(token_count, top_count)


def pickers_of(pair_slot, experts, capacity):
    flat = pair_slot.T.reshape(-1)
    slots = jnp.arange(experts * capacity, dtype=jnp.int32).reshape(experts, 1, capacity)
    return (flat[None, :, None] == slots).astype(BF16)


def inverse_of(values):
    return lax.rsqrt(jnp.mean(values * values, axis=-1, keepdims=True) + EPSILON)


def body(tokens, grad_out, norm_gain, expert_ids, gate_weights, w_gate, w_up, w_down):
    tokens = tokens[0]
    grad_rows = grad_out[0]
    gain = norm_gain[0][None, :]
    route_ids = expert_ids[0]
    route_weights = gate_weights[0]
    token_count, width = tokens.shape
    top_count = route_ids.shape[1]
    devices = lax.axis_size("expert")
    pipes = lax.axis_size("pipe")
    experts = devices // SLICES
    step_size = 4 * experts * SLICES
    capacity = min(
        token_count, SLICES * ((token_count * top_count * 5 + step_size - 1) // step_size)
    )
    home = lax.axis_index("expert") // SLICES
    same = lambda d: d

    gate, up, down = w_gate[0], w_up[0], w_down[0]

    if experts == 4 and token_count == LANES:
        next_rows, prev_rows = relay_layer(
            route_ids.T, route_weights.T, gain, gate, up, down, tokens, grad_rows, capacity, top_count
        )
        return (next_rows[None], prev_rows[None])

    values = tokens.astype(F32)
    inverse = inverse_of(values)
    pair_slot = slots_of(route_ids, home, experts, capacity)
    picker = jnp.any(
        pair_slot[None, :, :]
        == jnp.arange(experts * capacity, dtype=jnp.int32)[:, None, None],
        axis=2,
    ).astype(BF16)

    routing = jnp.concatenate([pair_slot.astype(F32), route_weights, inverse], axis=1)
    routing_next = move(routing, 1, same)
    routing_prev = routing_next if pipes == 2 else move(routing, -1, same)
    gain_prev = move(gain, -1, same)

    def routing_of(table):
        slots = table[:, :top_count].astype(jnp.int32)
        return pickers_of(slots, experts, capacity), table[:, top_count : 2 * top_count]

    pick_next, weights_next = routing_of(routing_next)
    pick_prev, weights_prev = routing_of(routing_prev)
    next_rows, prev_rows = layer(
        picker, inverse, gain, gate, up, down, tokens, grad_rows,
        gain_prev, routing_prev[:, 2 * top_count :],
        pick_next, weights_next, pick_prev, weights_prev,
    )
    return (next_rows[None], prev_rows[None])


def solution(mesh):
    return jax.shard_map(
        body,
        mesh=mesh,
        in_specs=(
            P("pipe", "expert", None),
            P("pipe", "expert", None),
            P("pipe", None),
            P("pipe", "expert", None),
            P("pipe", "expert", None),
            P("pipe", None, "expert"),
            P("pipe", None, "expert"),
            P("pipe", "expert", None),
        ),
        out_specs=(P("pipe", "expert", None), P("pipe", "expert", None)),
        check_vma=False,
    )
```
